32 devices in a mesh: grp: 2 (over y), lat: 4 (over z), lon: 2 (over x), comp: 2 (over core).
Axes of the slice: x: 2, y: 2, z: 4, core: 2. Of those that a mesh axis runs over, the one named last changes fastest.
Arguments:
- atmos_state: bfloat16 [48, 32, 768], P(None, ('grp', 'lat', 'comp'), 'lon'), parts along dimension 1, may hold values from -6 to 6
- ocean_state: bfloat16 [40, 32, 768], P(None, ('grp', 'lat', 'comp'), 'lon'), parts along dimension 1, may hold values from -6 to 6
- ocean_mask: int32 [32, 768], P(('grp', 'lat', 'comp'), 'lon'), parts along dimension 0, may hold values 0 or 1
- atmos_in_w: bfloat16 [2, 9, 256, 48], replicated, may hold values from -0.3125 to 0.3125
- atmos_out_w: bfloat16 [2, 9, 48, 256], replicated, may hold values from -0.125 to 0.125
- ocean_in_w: bfloat16 [2, 9, 128, 48], replicated, may hold values from -0.3125 to 0.3125
- ocean_out_w: bfloat16 [2, 9, 40, 128], replicated, may hold values from -0.1875 to 0.1875
- flux_proj: bfloat16 [8, 48], replicated, may hold values from -0.875 to 0.875
- regrid_blocks: bfloat16 [64, 128, 128], replicated, may hold values from -0.5 to 0.5
- regrid_source_block: int32 [16, 2, 8, 2], P(('grp', 'lat', 'comp'), 'lon'), parts along dimension 0, may hold values from -1 to 5, as said below
- regrid_target_block: int32 [16, 2, 8, 2], P(('grp', 'lat', 'comp'), 'lon'), parts along dimension 0, may hold values from 0 to 5
- regrid_weight_block: int32 [16, 2, 8, 2], P(('grp', 'lat', 'comp'), 'lon'), parts along dimension 0, may hold values from 0 to 63
Outputs:
- atmos_next: bfloat16 [48, 32, 768], P(None, ('grp', 'lat', 'comp'), 'lon'), parts along dimension 1
- ocean_next: bfloat16 [40, 32, 768], P(None, ('grp', 'lat', 'comp'), 'lon'), parts along dimension 1
- surface_temp_on_atmosphere: float32 [32, 768], P(('grp', 'lat', 'comp'), 'lon'), parts along dimension 0
The draws below stay inside these ranges and needn't reach their ends.
There are 2 independent parts, one for each index of `grp`. The reference program is written for one: setup_inputs(seed, part) draws one part's arguments, and reference() takes and returns one part's arrays. A program takes and returns all parts, laid end to end along the dimension named above; an argument that names none is the same for every part. Nothing has to cross between parts.
Inputs may be any that keep to these rules, and one draw needn't show every extreme that they name: `regrid_source_block`: empty slots hold -1, live ones a sub-block of the source tile; each tile has both slots to the next latitude tile (t + 1 modulo 8) live, and the share of live slots differs from one latitude tile to another.
All inputs are finite; a program needn't handle non-finite values. No bound on the sum of `ocean_mask` on one device may be relied on, other than what follows from the above.
Results may differ from the reference program's by a relative error of at most 0.02.
Values may be sent and summed in bfloat16 or wider, within the bound.
A program may use at most 64 MiB of HBM per device.

```python
import jax
import jax.numpy as jnp
from jax import lax

C_A = 48
HA = 256
C_O = 40
HO = 128
NF = 8
NB = 2
BC = 128
NW = 64
CAP = 2
RA = 2
WA = 384
NTL = 8
SB = 6
NLAT = 16
NLON = 768
N_LON = 2


def draw_regrid_source_block(key, part):
    key_blocks, key_rolls, key_rates = jax.random.split(key, 3)
    shape = (NTL, N_LON, NTL, CAP)
    blocks = jax.random.randint(key_blocks, shape, 0, SB)
    rolls = jax.random.randint(key_rolls, shape, 0, 8)
    rates = jax.random.randint(key_rates, (NTL, 1, 1, 1), 2, 8)
    source_ids = jnp.arange(NTL, dtype=jnp.int32)[:, None, None, None]
    neighbor_index = jnp.arange(NTL, dtype=jnp.int32)[None, None, :, None]
    forced = neighbor_index == (source_ids + 1) % NTL
    live = (rolls < rates) | forced
    return jnp.where(live, blocks, -1).astype(jnp.int32)


def plant(drawn, rng, smallest, largest):
    longest = drawn.shape.index(max(drawn.shape))
    spots = []
    for shift in (0, 1):
        where = [jax.random.randint(jax.random.fold_in(rng, axis), (), 0, length) for axis, length in enumerate(drawn.shape)]
        where[longest] = (where[longest] + shift) % drawn.shape[longest]
        spots.append(tuple(where))
    return drawn.at[spots[0]].set(smallest).at[spots[1]].set(largest)


def block_levels(rng, dims, cuts, smallest, largest):
    gain, own = 1.0, jax.random.fold_in(rng, 6)
    for dim, shards_of in cuts:
        draws = jnp.exp(jax.random.uniform(jax.random.fold_in(own, dim), (shards_of,), jnp.float32, smallest / len(cuts), largest / len(cuts)))
        gain = gain * jnp.repeat(draws, dims[dim] // shards_of).reshape([-1 if axis == dim else 1 for axis in range(len(dims))])
    return gain


def noise(own_key, extent, scale, limit, shards=(), held_as=jnp.bfloat16):
    result = jax.random.normal(own_key, extent, jnp.float32) * scale
    if len(shards) > 0:
        result = block_levels(own_key, extent, shards, -0.22, 0.18) * result
    return jnp.clip(result, min=-limit, max=limit).astype(held_as)


def setup_inputs(seed: int = 0, part: int = 0) -> dict:
    streams_of = jax.random.split(jax.random.key(seed), 13)
    own_keys = jax.random.split(jax.random.fold_in(streams_of[12], part), 13)
    return {
        "atmos_state": noise(own_keys[0], (C_A, NLAT, NLON), 1.0, 6.0, ((1, 8), (2, 2))),
        "ocean_state": noise(own_keys[1], (C_O, NLAT, NLON), 1.0, 6.0, ((1, 8), (2, 2))),
        "ocean_mask": plant((jax.random.randint(own_keys[2], (NLAT, NLON), 0, 3) < 2).astype(jnp.int32), jax.random.fold_in(own_keys[2], 1), 0, 1),
        "atmos_in_w": noise(streams_of[3], (NB, 9, HA, C_A), (9 * C_A) ** -0.5, 0.3125),
        "atmos_out_w": noise(streams_of[4], (NB, 9, C_A, HA), (9 * HA) ** -0.5, 0.125),
        "ocean_in_w": noise(streams_of[5], (NB, 9, HO, C_O + NF), (9 * (C_O + NF)) ** -0.5, 0.3125),
        "ocean_out_w": noise(streams_of[6], (NB, 9, C_O, HO), (9 * HO) ** -0.5, 0.1875),
        "flux_proj": noise(streams_of[7], (NF, C_A), C_A ** -0.5, 0.875),
        "regrid_blocks": noise(streams_of[8], (NW, BC, BC), BC ** -0.5, 0.5),
        "regrid_source_block": draw_regrid_source_block(jax.random.fold_in(jax.random.fold_in(streams_of[12], part), 71), part),
        "regrid_target_block": plant(jax.random.randint(own_keys[10], (NTL, N_LON, NTL, CAP), 0, SB), jax.random.fold_in(own_keys[10], 1), 0, SB - 1).astype(jnp.int32),
        "regrid_weight_block": plant(jax.random.randint(own_keys[11], (NTL, N_LON, NTL, CAP), 0, NW), jax.random.fold_in(own_keys[11], 1), 0, NW - 1).astype(jnp.int32),
    }


def conv_field(field, taps):
    block_height, block_breadth = field.shape[1], field.shape[2]
    padded = jnp.pad(field.astype(jnp.float32), ((0, 0), (1, 1), (0, 0)))
    padded = jnp.concatenate([padded[:, :, -1:], padded, padded[:, :, :1]], axis=2)
    total = jnp.zeros((taps.shape[1], block_height, block_breadth), jnp.float32)
    for row_tap in range(3):
        for col_tap in range(3):
            window = padded[:, row_tap:row_tap + block_height, col_tap:col_tap + block_breadth]
            total = total + jnp.einsum("hc,crw->hrw", taps[row_tap * 3 + col_tap].astype(jnp.float32), window)
    return total


def conv_block(state, extra, w_in, w_out, wet):
    source = state if extra is None else jnp.concatenate([state, extra], axis=0)
    hidden = jax.nn.gelu(conv_field(source, w_in)).astype(jnp.bfloat16)
    total = state.astype(jnp.float32) + conv_field(hidden, w_out)
    if wet is not None:
        total = total * wet
    return total.astype(jnp.bfloat16)


def grid_into_tiles(field):
    chans = field.shape[0]
    tiles = field.reshape(chans, NTL, RA, N_LON, WA).transpose(1, 3, 0, 2, 4)
    return tiles.reshape(NTL, N_LON, chans, SB, BC)


def tiles_into_grid(tiles):
    chans = tiles.shape[2]
    grid = tiles.reshape(NTL, N_LON, chans, RA, WA).transpose(2, 0, 3, 1, 4)
    return grid.reshape(chans, NTL * RA, N_LON * WA)


def pick_blocks(tiles_lon, index_lon):
    return jnp.take(tiles_lon, index_lon, axis=1)


def reference(atmos_state, ocean_state, ocean_mask, atmos_in_w, atmos_out_w, ocean_in_w, ocean_out_w, flux_proj, regrid_blocks, regrid_source_block, regrid_target_block, regrid_weight_block):
    atmosphere_model = atmos_state
    for layer in range(NB):
        atmosphere_model = conv_block(atmosphere_model, None, atmos_in_w[layer], atmos_out_w[layer], None)
    surface_flux = jnp.einsum("fc,crw->frw", flux_proj.astype(jnp.float32), atmosphere_model.astype(jnp.float32)).astype(jnp.bfloat16)
    flux_tiles = grid_into_tiles(surface_flux).astype(jnp.float32)
    blocks_wide = regrid_blocks.astype(jnp.float32)
    neighbor_index = jnp.arange(NTL, dtype=jnp.int32)[None, :, None]
    longitude_index = jnp.arange(N_LON, dtype=jnp.int32)[:, None, None]

    def send_step(carry, inputs):
        tiles_src, sources, destination_blocks, weights_idx = inputs
        live = sources >= 0
        clipped = jnp.maximum(sources, 0).astype(jnp.int32)
        chosen = jax.vmap(pick_blocks)(tiles_src, clipped)
        collected_values = blocks_wide[weights_idx]
        contrib = jnp.einsum("lfpcb,lpcbd->lpcfd", chosen, collected_values)
        contrib = jnp.where(live[..., None, None], contrib, jnp.zeros((), jnp.float32))
        contrib = lax.optimization_barrier(contrib.astype(jnp.bfloat16)).astype(jnp.float32)
        carry = carry.at[neighbor_index, longitude_index, destination_blocks.astype(jnp.int32)].add(contrib)
        return carry, None

    start = jnp.zeros((NTL, N_LON, SB, NF, BC), jnp.float32)
    received, unused = lax.scan(send_step, start, (flux_tiles, regrid_source_block, regrid_target_block, regrid_weight_block))
    ocean_flux = tiles_into_grid(received.transpose(0, 1, 3, 2, 4)).astype(jnp.bfloat16)

    wet = ocean_mask.astype(jnp.float32)[None]
    ocean_model = (ocean_state.astype(jnp.float32) * wet).astype(jnp.bfloat16)
    for layer in range(NB):
        ocean_model = conv_block(ocean_model, ocean_flux, ocean_in_w[layer], ocean_out_w[layer], wet)

    surface_temp_tile = grid_into_tiles(ocean_model[0:1])[:, :, 0].astype(jnp.float32)

    def return_exchange(carry, inputs):
        sources, destination_blocks, weights_idx = inputs
        live = sources >= 0
        clipped = jnp.maximum(sources, 0).astype(jnp.int32)
        block_values = surface_temp_tile[neighbor_index, longitude_index, destination_blocks.astype(jnp.int32)]
        collected_values = blocks_wide[weights_idx]
        contrib = jnp.einsum("lpcbd,lpcd->lpcb", collected_values, block_values)
        contrib = jnp.where(live[..., None], contrib, jnp.zeros((), jnp.float32))
        local = jnp.zeros((N_LON, SB, BC), jnp.float32).at[longitude_index, clipped].add(contrib)
        return carry, local

    discarded_second, surface_temp_pieces = lax.scan(return_exchange, jnp.zeros((), jnp.float32), (regrid_source_block, regrid_target_block, regrid_weight_block))
    surface_temp_on_atmosphere = tiles_into_grid(surface_temp_pieces[:, :, None])[0]
    return atmosphere_model, ocean_model, surface_temp_on_atmosphere
```

```python
import functools

import jax
import jax.numpy as jnp
from jax import lax
from jax.experimental import pallas as pl
from jax.experimental.pallas import tpu as pltpu
from jax.sharding import PartitionSpec as P

MESH = pl.DeviceIdType.MESH
F32 = jnp.float32
BF16 = jnp.bfloat16
WIDE = 512


def gelu(v, keep):
    half = (0.5 * keep) * v
    return half + half * jnp.tanh(v * (0.7978845608 + (0.7978845608 * 0.044715) * (v * v)))


def kernel(
    dims,
    src_hbm,
    tgt_hbm,
    wgt_hbm,
    atmos_hbm,
    ocean_hbm,
    mask_hbm,
    proj_hbm,
    ain_hbm,
    aout_hbm,
    oin_hbm,
    oout_hbm,
    blk_hbm,
    anext_ref,
    onext_ref,
    temp_ref,
    src_ref,
    tgt_ref,
    wgt_ref,
    atmos_ref,
    ocean_ref,
    mask_ref,
    proj_ref,
    ain_v,
    aout_v,
    oin_v,
    oout_v,
    blk_v,
    wa_in,
    wa_out,
    wo_in,
    wo_out,
    main,
    rim,
    edge,
    xp,
    xf,
    pre,
    wo_flux,
    hid,
    ohid,
    st,
    fmain,
    fedge_src,
    fedge,
    tq_src,
    tq,
    cs,
    cr,
    bs,
    br,
    w_sem,
    i_sem,
    ms,
    mr,
    es,
    er,
    fms,
    fmr,
    fes,
    fer,
    tqs,
    tqr,
    c_s,
    c_r,
    b_s,
    b_r,
):
    nt, nc, nl = dims
    comp = lax.axis_index("comp")
    lat = lax.axis_index("lat")
    lon = lax.axis_index("lon")
    t = lat * nc + comp
    sides = (1,) if nl == 2 else (1, nl - 1)

    def dev(tt, ll):
        return {"lat": lax.div(tt, nc), "comp": lax.rem(tt, nc), "lon": ll}

    def inside(d):
        return (t + d >= 0) & (t + d < nt)

    barrier = pltpu.get_barrier_semaphore()
    for k in range(1, nt):
        pl.semaphore_signal(
            barrier, inc=1, device_id=dev(lax.rem(t + k, nt), lon), device_id_type=MESH
        )
    for e in range(-2, 3):

        @pl.when(inside(e))
        def _():
            for s in sides:
                pl.semaphore_signal(
                    barrier,
                    inc=1,
                    device_id=dev(t + e, lax.rem(lon + s, nl)),
                    device_id_type=MESH,
                )

    input_copies = [
        pltpu.make_async_copy(src, dst, i_sem.at[i])
        for i, (src, dst) in enumerate(
            (
                (atmos_hbm, atmos_ref),
                (tgt_hbm, tgt_ref),
                (ocean_hbm, ocean_ref),
                (mask_hbm, mask_ref),
                (src_hbm, src_ref),
                (wgt_hbm, wgt_ref),
                (proj_hbm, proj_ref),
            )
        )
    ]
    for copy in input_copies:
        copy.start()
    weight_copies = [
        pltpu.make_async_copy(src, dst, w_sem.at[i])
        for i, (src, dst) in enumerate(
            (
                (ain_hbm, ain_v),
                (aout_hbm, aout_v),
                (blk_hbm, blk_v),
                (oin_hbm, oin_v),
                (oout_hbm, oout_v),
            )
        )
    ]
    for copy in weight_copies:
        copy.start()
    lane = lax.broadcasted_iota(jnp.int32, (16, 128), 1)

    def own_tile(m, rows):
        packed = jnp.zeros((16, 128), F32)
        for i in range(2):
            main[m, 2, i] = rows[i].astype(BF16)
            for g in range(3):
                q = i * 3 + g
                part = rows[i][16 * g : 16 * g + 16]
                ends = jnp.where(lane < 64, part[:, 0:128], part[:, 256:384])
                moved = pltpu.roll(ends, 16 * q + 8, 1)
                packed = jnp.where((lane >= 16 * q) & (lane < 16 * q + 16), moved, packed)
        rim[m] = packed.astype(BF16)

    input_copies[0].wait()
    own_tile(0, [atmos_ref[:, i, :].astype(F32) for i in range(2)])
    input_copies[1].wait()
    for p in range(nt):
        tq_src[p] = jnp.concatenate(
            [jnp.full((8, 128), tgt_ref[s, p], jnp.int32) for s in range(2)], axis=0
        ).astype(F32).astype(BF16)
    for copy in input_copies[2:]:
        copy.wait()
    wet = mask_ref[...].astype(F32)
    own_tile(
        1,
        [
            jnp.concatenate(
                [
                    ocean_ref[:, i, :].astype(F32) * wet[i : i + 1],
                    jnp.broadcast_to(wet[i : i + 1], (8, 384)),
                ],
                axis=0,
            )
            for i in range(2)
        ],
    )
    low = jnp.minimum(t, 2)
    high = jnp.minimum(nt - 1 - t, 2)
    pl.semaphore_wait(barrier, nt - 1 + len(sides) * (low + high + 1))

    def exchange(main_src, main_dst, edge_src, edge_dst, msend, mrecv, esend, erecv):
        def main_copy(e, out):
            j = 2 - e if out else e + 2
            return pltpu.make_async_remote_copy(
                src_ref=main_src,
                dst_ref=main_dst.at[j],
                send_sem=msend.at[e + 2],
                recv_sem=mrecv.at[j],
                device_id=dev(t + e, lon),
                device_id_type=MESH,
            )

        def edge_copy(e, n, s, out):
            j = 2 - e if out else e + 2
            return pltpu.make_async_remote_copy(
                src_ref=edge_src,
                dst_ref=edge_dst.at[n, j],
                send_sem=esend.at[n, e + 2],
                recv_sem=erecv.at[n, j],
                device_id=dev(t + e, lax.rem(lon + s, nl)),
                device_id_type=MESH,
            )

        def start():
            for e in (-2, 2, -1, 1, 0):

                @pl.when(inside(e))
                def _():
                    if e != 0:
                        main_copy(e, True).start()
                    for n, s in enumerate(sides):
                        edge_copy(e, n, s, True).start()

        def wait_recv():
            for d in (0, 1, -1, 2, -2):

                @pl.when(inside(d))
                def _():
                    for n, s in enumerate(sides):
                        edge_copy(d, n, s, False).wait_recv()
                    if d != 0:
                        main_copy(d, False).wait_recv()

                if d != 0:

                    @pl.when(jnp.logical_not(inside(d)))
                    def _():
                        main_dst[d + 2] = jnp.zeros(main_dst.shape[1:], main_dst.dtype)
                        for n in range(len(sides)):
                            edge_dst[n, d + 2] = jnp.zeros(edge_dst.shape[2:], edge_dst.dtype)

        def wait_send():
            for e in (-2, 2, -1, 1, 0):

                @pl.when(inside(e))
                def _():
                    if e != 0:
                        main_copy(e, True).wait_send()
                    for n, s in enumerate(sides):
                        edge_copy(e, n, s, True).wait_send()

        return start, wait_recv, wait_send

    def swap(src, dst, ssem, rsem):
        def copy(p, out):
            return pltpu.make_async_remote_copy(
                src_ref=src.at[p],
                dst_ref=dst.at[t if out else p],
                send_sem=ssem.at[p],
                recv_sem=rsem.at[t if out else p],
                device_id=dev(jnp.int32(p), lon),
                device_id_type=MESH,
            )

        def start(p):
            @pl.when(t != p)
            def _():
                copy(p, True).start()

            @pl.when(t == p)
            def _():
                dst[p] = src[p]

        def wait_recv(p):
            @pl.when(t != p)
            def _():
                copy(p, False).wait_recv()

        def wait_send():
            for p in range(nt):

                @pl.when(t != p)
                def _():
                    copy(p, True).wait_send()

        return start, wait_recv, wait_send

    halos = [
        exchange(
            main.at[m, 2],
            main.at[m],
            rim.at[m],
            edge.at[m],
            ms.at[m],
            mr.at[m],
            es.at[m],
            er.at[m],
        )
        for m in range(2)
    ]
    halos[0][0]()
    tq_start, tq_wait, tq_done = swap(tq_src, tq, tqs, tqr)
    for p in range(nt):
        tq_start(p)

    def stack_in(src, dst):
        for k in range(2):
            dst[k] = src[k].reshape(432, src.shape[3]).T

    def stack_out(src, dst, c, h):
        for k in range(2):
            for a in range(3):
                for b in range(3):
                    dst[k, b * 48 : b * 48 + c, a * h : (a + 1) * h] = src[k, 3 * a + b]

    weight_copies[0].wait()
    stack_in(ain_v, wa_in)
    weight_copies[1].wait()
    stack_out(aout_v, wa_out, 48, 256)

    def valid(r):
        row = 2 * t + r - 4
        return (row >= 0) & (row < 2 * nt)

    def wide_row(m, r):
        j, i = r // 2, r % 2
        pieces = []
        for g in range(3):
            shift = (120 - (i * 3 + g) * 16) % 128
            got = [pltpu.roll(edge[m, n, j].astype(F32), shift, 1) for n in range(len(sides))]
            pieces.append(got[0] if len(got) == 1 else jnp.where(lane < 64, got[1], got[0]))
        return jnp.concatenate(
            [main[m, j, i].astype(F32), jnp.concatenate(pieces, axis=0)], axis=1
        )

    def put_taps(r, row):
        xp[r, 0:48] = pltpu.roll(row, 1, 1).astype(BF16)
        xp[r, 48:96] = row.astype(BF16)
        xp[r, 96:144] = pltpu.roll(row, WIDE - 1, 1).astype(BF16)

    def conv_in(w, buf, r):
        patch = xp[pl.ds(r - 1, 3)].reshape(432, WIDE)
        v = jnp.dot(w, patch, preferred_element_type=F32)
        buf[r - 1] = gelu(v, jnp.where(valid(r), 1.0, 0.0)).astype(BF16)

    def conv_out(w, buf, r):
        h = buf.shape[1]
        y = jnp.dot(w, buf[pl.ds(r - 2, 3)].reshape(3 * h, WIDE), preferred_element_type=F32)
        return pltpu.roll(y[0:48], 1, 1) + y[48:96] + pltpu.roll(y[96:144], WIDE - 1, 1)

    def loop(lo, hi, fn):
        for r in range(lo, hi):
            fn(r)

    halos[0][1]()
    halos[1][0]()
    for r in range(10):
        row = wide_row(0, r)
        put_taps(r, row)
        if 2 <= r < 8:
            st[r] = row

    arows, orows = [], []
    for layer in range(2):
        first = 1 + 2 * layer

        loop(first, 10 - first, lambda r: conv_in(wa_in[layer], hid, r))
        for r in range(first + 1, 9 - first):
            row = (st[r] + conv_out(wa_out[layer], hid, r)).astype(BF16)
            if layer == 0:
                row = row.astype(F32) * jnp.where(valid(r), 1.0, 0.0)
                st[r] = row
                put_taps(r, row)
            else:
                arows.append(row[:, 0:384])

    flux = [
        jnp.dot(proj_ref[...], arows[i], preferred_element_type=F32).astype(BF16).astype(F32)
        for i in range(2)
    ]
    sub = [flux[b // 3][:, (b % 3) * 128 : (b % 3 + 1) * 128] for b in range(6)]
    weight_copies[2].wait()
    c_start, c_wait, c_done = swap(cs, cr, c_s, c_r)
    for p in range(nt):
        out = []
        for s in range(2):
            source = jnp.full((8, 128), src_ref[s, p], jnp.int32)
            chosen = jnp.zeros((8, 128), F32)
            for b in range(6):
                chosen = jnp.where(source == b, sub[b], chosen)
            out.append(
                jnp.dot(
                    chosen.astype(BF16),
                    blk_v[wgt_ref[s, p]],
                    preferred_element_type=F32,
                )
            )
        cs[p] = jnp.concatenate(out, axis=0).astype(BF16)
        c_start(p)

    anext_ref[...] = jnp.stack([v.astype(F32) for v in arows], axis=1).astype(BF16)
    weight_copies[3].wait()
    stack_in(oin_v, wo_in)
    weight_copies[4].wait()
    wo_out[...] = jnp.zeros(wo_out.shape, BF16)
    stack_out(oout_v, wo_out, 40, 128)
    halos[1][1]()
    taps = [oin_v[0, tap].astype(F32)[40:48] for tap in range(9)]
    gap = [jnp.zeros((8, 128), F32)]
    wo_flux[...] = (
        jnp.concatenate(taps[0:3] + gap + taps[3:6] + gap + taps[6:9] + gap, axis=0).astype(BF16).T
    )
    for r in range(10):
        row = wide_row(1, r)
        st[r] = row
        put_taps(r, jnp.concatenate([row[0:40], jnp.zeros((8, WIDE), F32)], axis=0))

    def pre_in(r):
        patch = xp[r - 1 : r + 2].reshape(432, WIDE)
        pre[r - 1] = jnp.dot(wo_in[0], patch, preferred_element_type=F32)

    for r in range(1, 5):
        pre_in(r)
    for p in range(nt):
        tq_wait(p)

    total = [jnp.zeros((8, 128), F32) for b in range(6)]
    for p in range(nt):
        c_wait(p)
        arrived = cr[p].astype(F32)
        target = tq[p].astype(F32)
        for s in range(2):
            value, where_to = arrived[8 * s : 8 * s + 8], target[8 * s : 8 * s + 8]
            for b in range(6):
                total[b] = total[b] + jnp.where(where_to == b, value, 0.0)
    own = jnp.concatenate(
        [jnp.concatenate(total[0:3], axis=1), jnp.concatenate(total[3:6], axis=1)], axis=0
    )
    fmain[2] = own.astype(BF16)
    fedge_src[...] = jnp.where(lane < 64, own[:, 0:128], own[:, 256:384]).astype(BF16)
    f_start, f_wait, f_done = exchange(
        fmain.at[2], fmain, fedge_src, fedge, fms, fmr, fes, fer
    )
    f_start()
    for r in range(5, 9):
        pre_in(r)
    f_wait()

    def flux_row(r):
        j, i = r // 2, r % 2
        got = [fedge[n, j].astype(F32) for n in range(len(sides))]
        side = got[0] if len(got) == 1 else jnp.where(lane < 64, got[1], got[0])
        both = jnp.concatenate([fmain[j].astype(F32), side], axis=1)
        return both[8 * i : 8 * i + 8]

    for r in range(10):
        row = flux_row(r)
        xf[r] = jnp.concatenate(
            [
                pltpu.roll(row, 1, 1),
                row,
                pltpu.roll(row, WIDE - 1, 1),
                jnp.zeros((8, WIDE), F32),
            ],
            axis=0,
        ).astype(BF16)
    temp = None

    def flux_in(r):
        v = pre[r - 1] + jnp.dot(
            wo_flux[...], xf[r - 1 : r + 2].reshape(96, WIDE), preferred_element_type=F32
        )
        ohid[r - 1] = gelu(v, jnp.where(valid(r), 1.0, 0.0)).astype(BF16)
    for layer in range(2):
        first = 1 + 2 * layer

        if layer == 0:
            loop(1, 9, flux_in)
        else:
            loop(first, 10 - first, lambda r: conv_in(wo_in[layer], ohid, r))
        rows = []
        for r in range(first + 1, 9 - first):
            y = conv_out(wo_out[layer], ohid, r)
            row = ((st[r, 0:40] + y[0:40]) * st[r, 40:41]).astype(BF16)
            if layer == 0:
                row = row.astype(F32) * jnp.where(valid(r), 1.0, 0.0)
                st[r, 0:40] = row
                put_taps(r, jnp.concatenate([row, flux_row(r)], axis=0))
            else:
                orows.append(row[:, 0:384])
                rows.append(row[0:16, 0:384].astype(F32)[0:1])
        temp = rows

    warm = [
        jnp.broadcast_to(temp[b // 3][:, (b % 3) * 128 : (b % 3 + 1) * 128], (16, 128))
        for b in range(6)
    ]
    b_start, b_wait, b_done = swap(bs, br, b_s, b_r)
    for p in range(nt):
        target = tq[p].astype(F32)
        back = jnp.zeros((16, 128), F32)
        for b in range(6):
            back = jnp.where(target == b, warm[b], back)
        bs[p] = back.astype(BF16)
        b_start(p)
    onext_ref[...] = jnp.stack([v.astype(F32) for v in orows], axis=1).astype(BF16)
    heat = [jnp.zeros((8, 128), F32) for b in range(6)]
    for p in range(nt):
        b_wait(p)
        got = br[p].astype(F32)
        for s in range(2):
            piece = lax.dot_general(
                got[8 * s : 8 * s + 8].astype(BF16),
                blk_v[wgt_ref[s, p]],
                (((1,), (1,)), ((), ())),
                preferred_element_type=F32,
            )
            source = jnp.full((8, 128), src_ref[s, p], jnp.int32)
            for b in range(6):
                heat[b] = heat[b] + jnp.where(source == b, piece, 0.0)
    for b in range(6):
        temp_ref[b // 3 : b // 3 + 1, (b % 3) * 128 : (b % 3 + 1) * 128] = heat[b][0:1]

    halos[0][2]()
    halos[1][2]()
    tq_done()
    c_done()
    f_done()
    b_done()


def hand_out_kernel(*refs):
    sems = refs[6]
    copies = [
        pltpu.make_async_copy(source, target, sems.at[i])
        for i, (source, target) in enumerate(zip(refs[:3], refs[3:6]))
    ]
    for copy in copies:
        copy.start()
    for copy in copies:
        copy.wait()


def hand_out(*arrays):
    vmem = pl.BlockSpec(memory_space=pltpu.VMEM)
    return pl.pallas_call(
        hand_out_kernel,
        out_shape=tuple(jax.ShapeDtypeStruct(v.shape, v.dtype) for v in arrays),
        in_specs=[vmem] * 3,
        out_specs=(pl.BlockSpec(memory_space=pltpu.HBM),) * 3,
        scratch_shapes=[pltpu.SemaphoreType.DMA((3,))],
    )(*[pltpu.with_memory_space_constraint(v, pltpu.VMEM) for v in arrays])


def per_device(
    dims,
    atmos_state,
    ocean_state,
    ocean_mask,
    atmos_in_w,
    atmos_out_w,
    ocean_in_w,
    ocean_out_w,
    flux_proj,
    regrid_blocks,
    regrid_source_block,
    regrid_target_block,
    regrid_weight_block,
):
    nt, nc, nl = dims
    sides = 1 if nl == 2 else 2
    in_taps = [w.transpose(0, 1, 3, 2) for w in (atmos_in_w, ocean_in_w)]
    links = [
        v.reshape(nt, 2).T
        for v in (regrid_source_block, regrid_target_block, regrid_weight_block)
    ]
    vmem = pl.BlockSpec(memory_space=pltpu.VMEM)
    hbm = pl.BlockSpec(memory_space=pltpu.HBM)
    dma = pltpu.SemaphoreType.DMA
    anext, onext, temp = pl.pallas_call(
        functools.partial(kernel, dims),
        out_shape=(
            pltpu.VMEM((48, 2, 384), BF16),
            pltpu.VMEM((40, 2, 384), BF16),
            pltpu.VMEM((2, 384), F32),
        ),
        in_specs=[hbm] * 12,
        out_specs=(vmem, vmem, vmem),
        scratch_shapes=[
            pltpu.SMEM((2, nt), jnp.int32),
            pltpu.SMEM((2, nt), jnp.int32),
            pltpu.SMEM((2, nt), jnp.int32),
            pltpu.VMEM(atmos_state.shape, BF16),
            pltpu.VMEM(ocean_state.shape, BF16),
            pltpu.VMEM(ocean_mask.shape, jnp.int32),
            pltpu.VMEM(flux_proj.shape, BF16),
            pltpu.VMEM(in_taps[0].shape, BF16),
            pltpu.VMEM(atmos_out_w.shape, BF16),
            pltpu.VMEM(in_taps[1].shape, BF16),
            pltpu.VMEM(ocean_out_w.shape, BF16),
            pltpu.VMEM(regrid_blocks.shape, BF16),
            pltpu.VMEM((2, 256, 432), BF16),
            pltpu.VMEM((2, 144, 768), BF16),
            pltpu.VMEM((2, 128, 432), BF16),
            pltpu.VMEM((2, 144, 384), BF16),
            pltpu.VMEM((2, 5, 2, 48, 384), BF16),
            pltpu.VMEM((2, 16, 128), BF16),
            pltpu.VMEM((2, sides, 5, 16, 128), BF16),
            pltpu.VMEM((10, 144, WIDE), BF16),
            pltpu.VMEM((10, 32, WIDE), BF16),
            pltpu.VMEM((8, 128, WIDE), F32),
            pltpu.VMEM((128, 96), BF16),
            pltpu.VMEM((8, 256, WIDE), BF16),
            pltpu.VMEM((8, 128, WIDE), BF16),
            pltpu.VMEM((10, 48, WIDE), F32),
            pltpu.VMEM((5, 16, 384), BF16),
            pltpu.VMEM((16, 128), BF16),
            pltpu.VMEM((sides, 5, 16, 128), BF16),
            pltpu.VMEM((nt, 16, 128), BF16),
            pltpu.VMEM((nt, 16, 128), BF16),
            pltpu.VMEM((nt, 16, 128), BF16),
            pltpu.VMEM((nt, 16, 128), BF16),
            pltpu.VMEM((nt, 16, 128), BF16),
            pltpu.VMEM((nt, 16, 128), BF16),
            dma((5,)),
            dma((7,)),
            dma((2, 5)),
            dma((2, 5)),
            dma((2, sides, 5)),
            dma((2, sides, 5)),
            dma((5,)),
            dma((5,)),
            dma((sides, 5)),
            dma((sides, 5)),
            dma((nt,)),
            dma((nt,)),
            dma((nt,)),
            dma((nt,)),
            dma((nt,)),
            dma((nt,)),
        ],
        compiler_params=pltpu.CompilerParams(
            collective_id=0, has_side_effects=True, vmem_limit_bytes=60 * 1024 * 1024
        ),
    )(
        *links,
        atmos_state,
        ocean_state,
        ocean_mask,
        flux_proj,
        in_taps[0],
        atmos_out_w,
        in_taps[1],
        ocean_out_w,
        regrid_blocks,
    )
    return hand_out(anext, onext, temp)


def solution(mesh):
    dims = (mesh.shape["lat"] * mesh.shape["comp"], mesh.shape["comp"], mesh.shape["lon"])
    field = P(None, ("grp", "lat", "comp"), "lon")
    plane = P(("grp", "lat", "comp"), "lon")
    links = P(("grp", "lat", "comp"), "lon", None, None)
    in_specs = (field, field, plane) + (P(),) * 6 + (links,) * 3
    return jax.shard_map(
        functools.partial(per_device, dims),
        mesh=mesh,
        in_specs=in_specs,
        out_specs=(field, field, plane),
        check_vma=False,
    )
```

```python
import functools

import jax
import jax.numpy as jnp
from jax import lax
from jax.experimental import pallas as pl
from jax.experimental.pallas import tpu as pltpu
from jax.sharding import PartitionSpec as P

MESH = pl.DeviceIdType.MESH
F32 = jnp.float32
BF16 = jnp.bfloat16
WIDE = 512
NEAR = (0, 1, -1)
FAR = (2, -2)


def gelu(v, keep):
    v = v.astype(BF16)
    half = (0.5 * keep).astype(BF16) * v
    slope = jnp.asarray(0.7978845608 * 0.044715, BF16) * (v * v)
    return half + half * jnp.tanh(v * (jnp.asarray(0.7978845608, BF16) + slope))


def kernel(
    dims,
    src_hbm,
    tgt_hbm,
    wgt_hbm,
    atmos_hbm,
    ocean_hbm,
    mask_hbm,
    proj_hbm,
    ain_hbm,
    aout_hbm,
    oin_hbm,
    oout_hbm,
    blk_hbm,
    anext_ref,
    onext_ref,
    temp_ref,
    src_ref,
    tgt_ref,
    wgt_ref,
    atmos_ref,
    ocean_ref,
    mask_ref,
    proj_ref,
    ain_v,
    aout_v,
    oin_v,
    oout_v,
    blk_v,
    wa_in,
    wa_out,
    wo_in,
    wo_out,
    main,
    rim,
    edge,
    xp,
    xf,
    pre,
    wo_flux,
    hid,
    ohid,
    st,
    fmain,
    fedge_src,
    fedge,
    tq_src,
    tq,
    cs,
    cr,
    bs,
    br,
    w_sem,
    i_sem,
    ms,
    mr,
    es,
    er,
    fms,
    fmr,
    fes,
    fer,
    tqs,
    tqr,
    c_s,
    c_r,
    b_s,
    b_r,
):
    nt, nc, nl = dims
    comp = lax.axis_index("comp")
    lat = lax.axis_index("lat")
    lon = lax.axis_index("lon")
    t = lat * nc + comp
    sides = (1,) if nl == 2 else (1, nl - 1)

    def dev(tt, ll):
        return {"lat": lax.div(tt, nc), "comp": lax.rem(tt, nc), "lon": ll}

    upper = lax.div(t, nt // 2)

    def near_first(i):
        return i + upper * (nt - 1 - 2 * i)

    def inside(d):
        return (t + d >= 0) & (t + d < nt)

    barrier = pltpu.get_barrier_semaphore()
    for k in range(1, nt):
        pl.semaphore_signal(
            barrier, inc=1, device_id=dev(lax.rem(t + k, nt), lon), device_id_type=MESH
        )
    for e in range(-2, 3):

        @pl.when(inside(e))
        def _():
            for s in sides:
                pl.semaphore_signal(
                    barrier,
                    inc=1,
                    device_id=dev(t + e, lax.rem(lon + s, nl)),
                    device_id_type=MESH,
                )

    input_copies = [
        pltpu.make_async_copy(src, dst, i_sem.at[i])
        for i, (src, dst) in enumerate(
            (
                (atmos_hbm, atmos_ref),
                (tgt_hbm, tgt_ref),
                (ocean_hbm, ocean_ref),
                (mask_hbm, mask_ref),
                (src_hbm, src_ref),
                (wgt_hbm, wgt_ref),
                (proj_hbm, proj_ref),
            )
        )
    ]
    for copy in input_copies:
        copy.start()
    weight_copies = [
        pltpu.make_async_copy(src, dst, w_sem.at[i])
        for i, (src, dst) in enumerate(
            (
                (ain_hbm, ain_v),
                (aout_hbm, aout_v),
                (blk_hbm, blk_v),
                (oin_hbm, oin_v),
                (oout_hbm, oout_v),
            )
        )
    ]
    for copy in weight_copies:
        copy.start()
    lane = lax.broadcasted_iota(jnp.int32, (16, 128), 1)

    def own_tile(m, rows):
        packed = jnp.zeros((16, 128), F32)
        for i in range(2):
            main[m, 2, i] = rows[i].astype(BF16)
            for g in range(3):
                q = i * 3 + g
                part = rows[i][16 * g : 16 * g + 16]
                ends = jnp.where(lane < 64, part[:, 0:128], part[:, 256:384])
                moved = pltpu.roll(ends, 16 * q + 8, 1)
                packed = jnp.where((lane >= 16 * q) & (lane < 16 * q + 16), moved, packed)
        rim[m] = packed.astype(BF16)

    input_copies[0].wait()
    own_tile(0, [atmos_ref[:, i, :].astype(F32) for i in range(2)])
    input_copies[1].wait()
    for p in range(nt):
        tq_src[p] = jnp.concatenate(
            [jnp.full((8, 128), tgt_ref[s, p], jnp.int32) for s in range(2)], axis=0
        ).astype(F32).astype(BF16)
    for copy in input_copies[2:]:
        copy.wait()
    wet = mask_ref[...].astype(F32)
    own_tile(
        1,
        [
            jnp.concatenate(
                [
                    ocean_ref[:, i, :].astype(F32) * wet[i : i + 1],
                    jnp.broadcast_to(wet[i : i + 1], (8, 384)),
                ],
                axis=0,
            )
            for i in range(2)
        ],
    )
    low = jnp.minimum(t, 2)
    high = jnp.minimum(nt - 1 - t, 2)
    pl.semaphore_wait(barrier, nt - 1 + len(sides) * (low + high + 1))

    def exchange(main_src, main_dst, edge_src, edge_dst, msend, mrecv, esend, erecv):
        def main_copy(e, out):
            j = 2 - e if out else e + 2
            return pltpu.make_async_remote_copy(
                src_ref=main_src,
                dst_ref=main_dst.at[j],
                send_sem=msend.at[e + 2],
                recv_sem=mrecv.at[j],
                device_id=dev(t + e, lon),
                device_id_type=MESH,
            )

        def edge_copy(e, n, s, out):
            j = 2 - e if out else e + 2
            return pltpu.make_async_remote_copy(
                src_ref=edge_src,
                dst_ref=edge_dst.at[n, j],
                send_sem=esend.at[n, e + 2],
                recv_sem=erecv.at[n, j],
                device_id=dev(t + e, lax.rem(lon + s, nl)),
                device_id_type=MESH,
            )

        def start():
            for e in (-1, 1, 0, -2, 2):

                @pl.when(inside(e))
                def _():
                    if e != 0:
                        main_copy(e, True).start()
                    for n, s in enumerate(sides):
                        edge_copy(e, n, s, True).start()

        def wait_recv(places):
            for d in places:

                @pl.when(inside(d))
                def _():
                    for n, s in enumerate(sides):
                        edge_copy(d, n, s, False).wait_recv()
                    if d != 0:
                        main_copy(d, False).wait_recv()

                if d != 0:

                    @pl.when(jnp.logical_not(inside(d)))
                    def _():
                        main_dst[d + 2] = jnp.zeros(main_dst.shape[1:], main_dst.dtype)
                        for n in range(len(sides)):
                            edge_dst[n, d + 2] = jnp.zeros(edge_dst.shape[2:], edge_dst.dtype)

        def wait_send():
            for e in (-2, 2, -1, 1, 0):

                @pl.when(inside(e))
                def _():
                    if e != 0:
                        main_copy(e, True).wait_send()
                    for n, s in enumerate(sides):
                        edge_copy(e, n, s, True).wait_send()

        return start, wait_recv, wait_send

    def swap(src, dst, ssem, rsem):
        def copy(p, out):
            return pltpu.make_async_remote_copy(
                src_ref=src.at[p],
                dst_ref=dst.at[t if out else p],
                send_sem=ssem.at[p],
                recv_sem=rsem.at[t if out else p],
                device_id=dev(jnp.int32(p), lon),
                device_id_type=MESH,
            )

        def start(p):
            @pl.when(t != p)
            def _():
                copy(p, True).start()

            @pl.when(t == p)
            def _():
                dst[p] = src[p]

        def wait_recv(p):
            @pl.when(t != p)
            def _():
                copy(p, False).wait_recv()

        def wait_send():
            for p in range(nt):

                @pl.when(t != p)
                def _():
                    copy(p, True).wait_send()

        return start, wait_recv, wait_send

    halos = [
        exchange(
            main.at[m, 2],
            main.at[m],
            rim.at[m],
            edge.at[m],
            ms.at[m],
            mr.at[m],
            es.at[m],
            er.at[m],
        )
        for m in range(2)
    ]
    halos[0][0]()
    tq_start, tq_wait, tq_done = swap(tq_src, tq, tqs, tqr)
    for i in range(nt):
        tq_start(near_first(i))

    def stack_in(src, dst):
        for k in range(2):
            dst[k] = src[k].reshape(432, src.shape[3]).T

    def stack_out(src, dst, c, h):
        for k in range(2):
            for a in range(3):
                for b in range(3):
                    dst[k, b * 48 : b * 48 + c, a * h : (a + 1) * h] = src[k, 3 * a + b]

    weight_copies[0].wait()
    stack_in(ain_v, wa_in)
    weight_copies[1].wait()
    stack_out(aout_v, wa_out, 48, 256)

    def valid(r):
        row = 2 * t + r - 4
        return (row >= 0) & (row < 2 * nt)

    def wide_row(m, r):
        j, i = r // 2, r % 2
        pieces = []
        for g in range(3):
            shift = (120 - (i * 3 + g) * 16) % 128
            got = [pltpu.roll(edge[m, n, j].astype(F32), shift, 1) for n in range(len(sides))]
            pieces.append(got[0] if len(got) == 1 else jnp.where(lane < 64, got[1], got[0]))
        return jnp.concatenate(
            [main[m, j, i].astype(F32), jnp.concatenate(pieces, axis=0)], axis=1
        )

    def put_taps(r, row):
        xp[r, 0:48] = pltpu.roll(row, 1, 1).astype(BF16)
        xp[r, 48:96] = row.astype(BF16)
        xp[r, 96:144] = pltpu.roll(row, WIDE - 1, 1).astype(BF16)

    def conv_in(w, buf, r):
        patch = xp[pl.ds(r - 1, 3)].reshape(432, WIDE)
        v = jnp.dot(w, patch, preferred_element_type=F32)
        buf[r - 1] = gelu(v, jnp.where(valid(r), 1.0, 0.0)).astype(BF16)

    def conv_out(w, buf, r):
        h = buf.shape[1]
        y = jnp.dot(w, buf[pl.ds(r - 2, 3)].reshape(3 * h, WIDE), preferred_element_type=F32)
        return pltpu.roll(y[0:48], 1, 1) + y[48:96] + pltpu.roll(y[96:144], WIDE - 1, 1)

    def loop(lo, hi, fn):
        for r in range(lo, hi):
            fn(r)

    def load_rows(rows):
        for r in rows:
            row = wide_row(0, r)
            put_taps(r, row)
            if 2 <= r < 8:
                st[r] = row

    halos[0][1](NEAR)
    load_rows(range(2, 8))
    loop(3, 7, lambda r: conv_in(wa_in[0], hid, r))
    halos[0][1](FAR)
    halos[1][0]()
    load_rows((0, 1, 8, 9))

    arows, orows = [], []
    for layer in range(2):
        first = 1 + 2 * layer

        for r in (1, 2, 7, 8) if layer == 0 else range(3, 7):
            conv_in(wa_in[layer], hid, r)
        for r in range(first + 1, 9 - first):
            row = (st[r] + conv_out(wa_out[layer], hid, r)).astype(BF16)
            if layer == 0:
                row = row.astype(F32) * jnp.where(valid(r), 1.0, 0.0)
                st[r] = row
                put_taps(r, row)
            else:
                arows.append(row[:, 0:384])

    flux = [
        jnp.dot(proj_ref[...], arows[i], preferred_element_type=F32).astype(BF16).astype(F32)
        for i in range(2)
    ]
    sub = [flux[b // 3][:, (b % 3) * 128 : (b % 3 + 1) * 128] for b in range(6)]
    weight_copies[2].wait()
    c_start, c_wait, c_done = swap(cs, cr, c_s, c_r)
    for i in range(nt):
        p = near_first(nt - 1 - i)
        out = []
        for s in range(2):
            source = jnp.full((8, 128), src_ref[s, p], jnp.int32)
            chosen = jnp.zeros((8, 128), F32)
            for b in range(6):
                chosen = jnp.where(source == b, sub[b], chosen)
            out.append(
                jnp.dot(
                    chosen.astype(BF16),
                    blk_v[wgt_ref[s, p]],
                    preferred_element_type=F32,
                )
            )
        cs[p] = jnp.concatenate(out, axis=0).astype(BF16)
        c_start(p)

    anext_ref[...] = jnp.stack([v.astype(F32) for v in arows], axis=1).astype(BF16)
    weight_copies[3].wait()
    stack_in(oin_v, wo_in)
    weight_copies[4].wait()
    wo_out[...] = jnp.zeros(wo_out.shape, BF16)
    stack_out(oout_v, wo_out, 40, 128)
    halos[1][1](NEAR + FAR)
    taps = [oin_v[0, tap].astype(F32)[40:48] for tap in range(9)]
    gap = [jnp.zeros((8, 128), F32)]
    wo_flux[...] = (
        jnp.concatenate(taps[0:3] + gap + taps[3:6] + gap + taps[6:9] + gap, axis=0).astype(BF16).T
    )
    for r in range(10):
        row = wide_row(1, r)
        st[r] = row
        put_taps(r, jnp.concatenate([row[0:40], jnp.zeros((8, WIDE), F32)], axis=0))

    def pre_in(r):
        patch = xp[r - 1 : r + 2].reshape(432, WIDE)
        pre[r - 1] = jnp.dot(wo_in[0], patch, preferred_element_type=F32)

    for r in range(1, 5):
        pre_in(r)
    for p in range(nt):
        tq_wait(p)

    total = [jnp.zeros((8, 128), F32) for b in range(6)]
    for p in range(nt):
        c_wait(p)
        arrived = cr[p].astype(F32)
        target = tq[p].astype(F32)
        for s in range(2):
            value, where_to = arrived[8 * s : 8 * s + 8], target[8 * s : 8 * s + 8]
            for b in range(6):
                total[b] = total[b] + jnp.where(where_to == b, value, 0.0)
    own = jnp.concatenate(
        [jnp.concatenate(total[0:3], axis=1), jnp.concatenate(total[3:6], axis=1)], axis=0
    )
    fmain[2] = own.astype(BF16)
    fedge_src[...] = jnp.where(lane < 64, own[:, 0:128], own[:, 256:384]).astype(BF16)
    f_start, f_wait, f_done = exchange(
        fmain.at[2], fmain, fedge_src, fedge, fms, fmr, fes, fer
    )
    f_start()
    for r in range(5, 9):
        pre_in(r)
    def flux_row(r):
        j, i = r // 2, r % 2
        got = [fedge[n, j].astype(F32) for n in range(len(sides))]
        side = got[0] if len(got) == 1 else jnp.where(lane < 64, got[1], got[0])
        both = jnp.concatenate([fmain[j].astype(F32), side], axis=1)
        return both[8 * i : 8 * i + 8]

    def flux_taps(rows):
        for r in rows:
            row = flux_row(r)
            xf[r] = jnp.concatenate(
                [
                    pltpu.roll(row, 1, 1),
                    row,
                    pltpu.roll(row, WIDE - 1, 1),
                    jnp.zeros((8, WIDE), F32),
                ],
                axis=0,
            ).astype(BF16)

    temp = None

    def flux_in(r):
        v = pre[r - 1] + jnp.dot(
            wo_flux[...], xf[r - 1 : r + 2].reshape(96, WIDE), preferred_element_type=F32
        )
        ohid[r - 1] = gelu(v, jnp.where(valid(r), 1.0, 0.0)).astype(BF16)
    for layer in range(2):
        first = 1 + 2 * layer

        if layer == 0:
            f_wait(NEAR)
            flux_taps(range(2, 8))
            loop(3, 7, flux_in)
            f_wait(FAR)
            flux_taps((0, 1, 8, 9))
            for r in (1, 2, 7, 8):
                flux_in(r)
        else:
            loop(first, 10 - first, lambda r: conv_in(wo_in[layer], ohid, r))
        rows = []
        for r in range(first + 1, 9 - first):
            y = conv_out(wo_out[layer], ohid, r)
            row = ((st[r, 0:40] + y[0:40]) * st[r, 40:41]).astype(BF16)
            if layer == 0:
                row = row.astype(F32) * jnp.where(valid(r), 1.0, 0.0)
                st[r, 0:40] = row
                put_taps(r, jnp.concatenate([row, flux_row(r)], axis=0))
            else:
                orows.append(row[:, 0:384])
                rows.append(row[0:16, 0:384].astype(F32)[0:1])
        temp = rows

    warm = [
        jnp.broadcast_to(temp[b // 3][:, (b % 3) * 128 : (b % 3 + 1) * 128], (16, 128))
        for b in range(6)
    ]
    b_start, b_wait, b_done = swap(bs, br, b_s, b_r)
    for i in range(nt):
        p = near_first(nt - 1 - i)
        target = tq[p].astype(F32)
        back = jnp.zeros((16, 128), F32)
        for b in range(6):
            back = jnp.where(target == b, warm[b], back)
        bs[p] = back.astype(BF16)
        b_start(p)
    onext_ref[...] = jnp.stack([v.astype(F32) for v in orows], axis=1).astype(BF16)
    heat = [jnp.zeros((8, 128), F32) for b in range(6)]
    for i in range(nt):
        p = near_first(i)
        b_wait(p)
        got = br[p].astype(F32)
        for s in range(2):
            piece = lax.dot_general(
                got[8 * s : 8 * s + 8].astype(BF16),
                blk_v[wgt_ref[s, p]],
                (((1,), (1,)), ((), ())),
                preferred_element_type=F32,
            )
            source = jnp.full((8, 128), src_ref[s, p], jnp.int32)
            for b in range(6):
                heat[b] = heat[b] + jnp.where(source == b, piece, 0.0)
    for b in range(6):
        temp_ref[b // 3 : b // 3 + 1, (b % 3) * 128 : (b % 3 + 1) * 128] = heat[b][0:1]

    halos[0][2]()
    halos[1][2]()
    tq_done()
    c_done()
    f_done()
    b_done()


def hand_out_kernel(*refs):
    sems = refs[6]
    copies = [
        pltpu.make_async_copy(source, target, sems.at[i])
        for i, (source, target) in enumerate(zip(refs[:3], refs[3:6]))
    ]
    for copy in copies:
        copy.start()
    for copy in copies:
        copy.wait()


def hand_out(*arrays):
    vmem = pl.BlockSpec(memory_space=pltpu.VMEM)
    return pl.pallas_call(
        hand_out_kernel,
        out_shape=tuple(jax.ShapeDtypeStruct(v.shape, v.dtype) for v in arrays),
        in_specs=[vmem] * 3,
        out_specs=(pl.BlockSpec(memory_space=pltpu.HBM),) * 3,
        scratch_shapes=[pltpu.SemaphoreType.DMA((3,))],
    )(*[pltpu.with_memory_space_constraint(v, pltpu.VMEM) for v in arrays])


def per_device(
    dims,
    atmos_state,
    ocean_state,
    ocean_mask,
    atmos_in_w,
    atmos_out_w,
    ocean_in_w,
    ocean_out_w,
    flux_proj,
    regrid_blocks,
    regrid_source_block,
    regrid_target_block,
    regrid_weight_block,
):
    nt, nc, nl = dims
    sides = 1 if nl == 2 else 2
    in_taps = [w.transpose(0, 1, 3, 2) for w in (atmos_in_w, ocean_in_w)]
    links = [
        v.reshape(nt, 2).T
        for v in (regrid_source_block, regrid_target_block, regrid_weight_block)
    ]
    vmem = pl.BlockSpec(memory_space=pltpu.VMEM)
    hbm = pl.BlockSpec(memory_space=pltpu.HBM)
    dma = pltpu.SemaphoreType.DMA
    anext, onext, temp = pl.pallas_call(
        functools.partial(kernel, dims),
        out_shape=(
            pltpu.VMEM((48, 2, 384), BF16),
            pltpu.VMEM((40, 2, 384), BF16),
            pltpu.VMEM((2, 384), F32),
        ),
        in_specs=[hbm] * 12,
        out_specs=(vmem, vmem, vmem),
        scratch_shapes=[
            pltpu.SMEM((2, nt), jnp.int32),
            pltpu.SMEM((2, nt), jnp.int32),
            pltpu.SMEM((2, nt), jnp.int32),
            pltpu.VMEM(atmos_state.shape, BF16),
            pltpu.VMEM(ocean_state.shape, BF16),
            pltpu.VMEM(ocean_mask.shape, jnp.int32),
            pltpu.VMEM(flux_proj.shape, BF16),
            pltpu.VMEM(in_taps[0].shape, BF16),
            pltpu.VMEM(atmos_out_w.shape, BF16),
            pltpu.VMEM(in_taps[1].shape, BF16),
            pltpu.VMEM(ocean_out_w.shape, BF16),
            pltpu.VMEM(regrid_blocks.shape, BF16),
            pltpu.VMEM((2, 256, 432), BF16),
            pltpu.VMEM((2, 144, 768), BF16),
            pltpu.VMEM((2, 128, 432), BF16),
            pltpu.VMEM((2, 144, 384), BF16),
            pltpu.VMEM((2, 5, 2, 48, 384), BF16),
            pltpu.VMEM((2, 16, 128), BF16),
            pltpu.VMEM((2, sides, 5, 16, 128), BF16),
            pltpu.VMEM((10, 144, WIDE), BF16),
            pltpu.VMEM((10, 32, WIDE), BF16),
            pltpu.VMEM((8, 128, WIDE), F32),
            pltpu.VMEM((128, 96), BF16),
            pltpu.VMEM((8, 256, WIDE), BF16),
            pltpu.VMEM((8, 128, WIDE), BF16),
            pltpu.VMEM((10, 48, WIDE), F32),
            pltpu.VMEM((5, 16, 384), BF16),
            pltpu.VMEM((16, 128), BF16),
            pltpu.VMEM((sides, 5, 16, 128), BF16),
            pltpu.VMEM((nt, 16, 128), BF16),
            pltpu.VMEM((nt, 16, 128), BF16),
            pltpu.VMEM((nt, 16, 128), BF16),
            pltpu.VMEM((nt, 16, 128), BF16),
            pltpu.VMEM((nt, 16, 128), BF16),
            pltpu.VMEM((nt, 16, 128), BF16),
            dma((5,)),
            dma((7,)),
            dma((2, 5)),
            dma((2, 5)),
            dma((2, sides, 5)),
            dma((2, sides, 5)),
            dma((5,)),
            dma((5,)),
            dma((sides, 5)),
            dma((sides, 5)),
            dma((nt,)),
            dma((nt,)),
            dma((nt,)),
            dma((nt,)),
            dma((nt,)),
            dma((nt,)),
        ],
        compiler_params=pltpu.CompilerParams(
            collective_id=0, has_side_effects=True, vmem_limit_bytes=60 * 1024 * 1024
        ),
    )(
        *links,
        atmos_state,
        ocean_state,
        ocean_mask,
        flux_proj,
        in_taps[0],
        atmos_out_w,
        in_taps[1],
        ocean_out_w,
        regrid_blocks,
    )
    return hand_out(anext, onext, temp)


def solution(mesh):
    dims = (mesh.shape["lat"] * mesh.shape["comp"], mesh.shape["comp"], mesh.shape["lon"])
    field = P(None, ("grp", "lat", "comp"), "lon")
    plane = P(("grp", "lat", "comp"), "lon")
    links = P(("grp", "lat", "comp"), "lon", None, None)
    in_specs = (field, field, plane) + (P(),) * 6 + (links,) * 3
    return jax.shard_map(
        functools.partial(per_device, dims),
        mesh=mesh,
        in_specs=in_specs,
        out_specs=(field, field, plane),
        check_vma=False,
    )
```

```python
import functools

import jax
import jax.numpy as jnp
from jax import lax
from jax.experimental import pallas as pl
from jax.experimental.pallas import tpu as pltpu
from jax.sharding import PartitionSpec as P

MESH = pl.DeviceIdType.MESH
F32 = jnp.float32
BF16 = jnp.bfloat16
WIDE = 512
NEAR = (0, 1, -1)
FAR = (2, -2)


def gelu(v, keep):
    v = v.astype(BF16)
    half = (0.5 * keep).astype(BF16) * v
    slope = jnp.asarray(0.7978845608 * 0.044715, BF16) * (v * v)
    return half + half * jnp.tanh(v * (jnp.asarray(0.7978845608, BF16) + slope))


def kernel(
    dims,
    src_hbm,
    tgt_hbm,
    wgt_hbm,
    atmos_hbm,
    ocean_hbm,
    mask_hbm,
    proj_hbm,
    ain_hbm,
    aout_hbm,
    oin_hbm,
    oout_hbm,
    blk_hbm,
    anext_ref,
    onext_ref,
    temp_ref,
    src_ref,
    tgt_ref,
    wgt_ref,
    atmos_ref,
    ocean_ref,
    mask_ref,
    proj_ref,
    ain_v,
    aout_v,
    oin_v,
    oout_v,
    blk_v,
    wa_in,
    wa_out,
    wo_in,
    wo_out,
    main,
    rim,
    edge,
    xp,
    xf,
    pre,
    wo_flux,
    hid,
    ohid,
    st,
    fmain,
    fedge_src,
    fedge,
    tq_src,
    tq,
    cs,
    cr,
    bs,
    br,
    w_sem,
    i_sem,
    ms,
    mr,
    es,
    er,
    fms,
    fmr,
    fes,
    fer,
    tqs,
    tqr,
    c_s,
    c_r,
    b_s,
    b_r,
):
    nt, nc, nl = dims
    comp = lax.axis_index("comp")
    lat = lax.axis_index("lat")
    lon = lax.axis_index("lon")
    t = lat * nc + comp
    sides = (1,) if nl == 2 else (1, nl - 1)

    def dev(tt, ll):
        return {"lat": lax.div(tt, nc), "comp": lax.rem(tt, nc), "lon": ll}

    upper = lax.div(t, nt // 2)

    def near_first(i):
        return i + upper * (nt - 1 - 2 * i)

    def inside(d):
        return (t + d >= 0) & (t + d < nt)

    barrier = pltpu.get_barrier_semaphore()
    for k in range(1, nt):
        pl.semaphore_signal(
            barrier, inc=1, device_id=dev(lax.rem(t + k, nt), lon), device_id_type=MESH
        )
    for e in range(-2, 3):

        @pl.when(inside(e))
        def _():
            for s in sides:
                pl.semaphore_signal(
                    barrier,
                    inc=1,
                    device_id=dev(t + e, lax.rem(lon + s, nl)),
                    device_id_type=MESH,
                )

    input_copies = [
        pltpu.make_async_copy(src, dst, i_sem.at[i])
        for i, (src, dst) in enumerate(
            (
                (atmos_hbm, atmos_ref),
                (tgt_hbm, tgt_ref),
                (ocean_hbm, ocean_ref),
                (mask_hbm, mask_ref),
                (src_hbm, src_ref),
                (wgt_hbm, wgt_ref),
                (proj_hbm, proj_ref),
            )
        )
    ]
    for copy in input_copies:
        copy.start()
    weight_copies = [
        pltpu.make_async_copy(src, dst, w_sem.at[i])
        for i, (src, dst) in enumerate(
            (
                (ain_hbm, ain_v),
                (aout_hbm, aout_v),
                (blk_hbm, blk_v),
                (oin_hbm, oin_v),
                (oout_hbm, oout_v),
            )
        )
    ]
    for copy in weight_copies:
        copy.start()
    lane = lax.broadcasted_iota(jnp.int32, (16, 128), 1)

    def own_rows(m, rows):
        for i in range(2):
            main[m, 2, i] = rows[i].astype(BF16)

    def own_rim(m, rows):
        packed = jnp.zeros((16, 128), F32)
        for i in range(2):
            for g in range(3):
                q = i * 3 + g
                part = rows[i][16 * g : 16 * g + 16]
                ends = jnp.where(lane < 64, part[:, 0:128], part[:, 256:384])
                moved = pltpu.roll(ends, 16 * q + 8, 1)
                packed = jnp.where((lane >= 16 * q) & (lane < 16 * q + 16), moved, packed)
        rim[m] = packed.astype(BF16)

    def exchange(main_src, main_dst, edge_src, edge_dst, msend, mrecv, esend, erecv):
        def main_copy(e, out):
            j = 2 - e if out else e + 2
            return pltpu.make_async_remote_copy(
                src_ref=main_src,
                dst_ref=main_dst.at[j],
                send_sem=msend.at[e + 2],
                recv_sem=mrecv.at[j],
                device_id=dev(t + e, lon),
                device_id_type=MESH,
            )

        def edge_copy(e, n, s, out):
            j = 2 - e if out else e + 2
            return pltpu.make_async_remote_copy(
                src_ref=edge_src,
                dst_ref=edge_dst.at[n, j],
                send_sem=esend.at[n, e + 2],
                recv_sem=erecv.at[n, j],
                device_id=dev(t + e, lax.rem(lon + s, nl)),
                device_id_type=MESH,
            )

        def start():
            for places in ((-1, 1, 0), (-2, 2)):
                for e in places:

                    @pl.when(inside(e))
                    def _():
                        for n, s in enumerate(sides):
                            edge_copy(e, n, s, True).start()

                for e in places:
                    if e != 0:

                        @pl.when(inside(e))
                        def _():
                            main_copy(e, True).start()

        def wait_recv(places):
            for d in places:

                @pl.when(inside(d))
                def _():
                    for n, s in enumerate(sides):
                        edge_copy(d, n, s, False).wait_recv()
                    if d != 0:
                        main_copy(d, False).wait_recv()

                if d != 0:

                    @pl.when(jnp.logical_not(inside(d)))
                    def _():
                        main_dst[d + 2] = jnp.zeros(main_dst.shape[1:], main_dst.dtype)
                        for n in range(len(sides)):
                            edge_dst[n, d + 2] = jnp.zeros(edge_dst.shape[2:], edge_dst.dtype)

        def wait_send():
            for e in (-2, 2, -1, 1, 0):

                @pl.when(inside(e))
                def _():
                    if e != 0:
                        main_copy(e, True).wait_send()
                    for n, s in enumerate(sides):
                        edge_copy(e, n, s, True).wait_send()

        return start, wait_recv, wait_send

    def swap(src, dst, ssem, rsem):
        def copy(p, out):
            return pltpu.make_async_remote_copy(
                src_ref=src.at[p],
                dst_ref=dst.at[t if out else p],
                send_sem=ssem.at[p],
                recv_sem=rsem.at[t if out else p],
                device_id=dev(jnp.int32(p), lon),
                device_id_type=MESH,
            )

        def start(p):
            @pl.when(t != p)
            def _():
                copy(p, True).start()

            @pl.when(t == p)
            def _():
                dst[p] = src[p]

        def wait_recv(p):
            @pl.when(t != p)
            def _():
                copy(p, False).wait_recv()

        def wait_send():
            for p in range(nt):

                @pl.when(t != p)
                def _():
                    copy(p, True).wait_send()

        return start, wait_recv, wait_send

    halos = [
        exchange(
            main.at[m, 2],
            main.at[m],
            rim.at[m],
            edge.at[m],
            ms.at[m],
            mr.at[m],
            es.at[m],
            er.at[m],
        )
        for m in range(2)
    ]
    input_copies[0].wait()
    atmos_rows = [atmos_ref[:, i, :].astype(F32) for i in range(2)]
    own_rows(0, atmos_rows)
    own_rim(0, atmos_rows)
    low = jnp.minimum(t, 2)
    high = jnp.minimum(nt - 1 - t, 2)
    pl.semaphore_wait(barrier, nt - 1 + len(sides) * (low + high + 1))
    halos[0][0]()
    input_copies[1].wait()
    for p in range(nt):
        tq_src[p] = jnp.concatenate(
            [jnp.full((8, 128), tgt_ref[s, p], jnp.int32) for s in range(2)], axis=0
        ).astype(F32).astype(BF16)
    for copy in input_copies[2:]:
        copy.wait()
    wet = mask_ref[...].astype(F32)
    ocean_rows = [
        jnp.concatenate(
            [
                ocean_ref[:, i, :].astype(F32) * wet[i : i + 1],
                jnp.broadcast_to(wet[i : i + 1], (8, 384)),
            ],
            axis=0,
        )
        for i in range(2)
    ]
    own_rows(1, ocean_rows)
    own_rim(1, ocean_rows)
    tq_start, tq_wait, tq_done = swap(tq_src, tq, tqs, tqr)
    for i in range(nt):
        tq_start(near_first(i))

    def stack_in(src, dst):
        for k in range(2):
            dst[k] = src[k].reshape(432, src.shape[3]).T

    def stack_out(src, dst, c, h):
        for k in range(2):
            for a in range(3):
                for b in range(3):
                    dst[k, b * 48 : b * 48 + c, a * h : (a + 1) * h] = src[k, 3 * a + b]

    weight_copies[0].wait()
    stack_in(ain_v, wa_in)
    weight_copies[1].wait()
    stack_out(aout_v, wa_out, 48, 256)

    def valid(r):
        row = 2 * t + r - 4
        return (row >= 0) & (row < 2 * nt)

    def wide_row(m, r):
        j, i = r // 2, r % 2
        pieces = []
        for g in range(3):
            shift = (120 - (i * 3 + g) * 16) % 128
            got = [pltpu.roll(edge[m, n, j].astype(F32), shift, 1) for n in range(len(sides))]
            pieces.append(got[0] if len(got) == 1 else jnp.where(lane < 64, got[1], got[0]))
        return jnp.concatenate(
            [main[m, j, i].astype(F32), jnp.concatenate(pieces, axis=0)], axis=1
        )

    def put_taps(r, row):
        row = row.astype(BF16)
        xp[r, 0:48] = pltpu.roll(row, 1, 1)
        xp[r, 48:96] = row
        xp[r, 96:144] = pltpu.roll(row, WIDE - 1, 1)

    def conv_in(w, buf, r):
        patch = xp[pl.ds(r - 1, 3)].reshape(432, WIDE)
        v = jnp.dot(w, patch, preferred_element_type=F32)
        buf[r - 1] = gelu(v, jnp.where(valid(r), 1.0, 0.0)).astype(BF16)

    def conv_out(w, buf, r):
        h = buf.shape[1]
        y = jnp.dot(w, buf[pl.ds(r - 2, 3)].reshape(3 * h, WIDE), preferred_element_type=F32)
        return pltpu.roll(y[0:48], 1, 1) + y[48:96] + pltpu.roll(y[96:144], WIDE - 1, 1)

    def loop(lo, hi, fn):
        for r in range(lo, hi):
            fn(r)

    def load_rows(rows):
        for r in rows:
            row = wide_row(0, r)
            put_taps(r, row)
            if 2 <= r < 8:
                st[r] = row

    halos[0][1](NEAR)
    load_rows(range(2, 8))
    loop(3, 7, lambda r: conv_in(wa_in[0], hid, r))
    halos[0][1](FAR)
    halos[1][0]()
    load_rows((0, 1, 8, 9))

    arows, orows = [], []
    for layer in range(2):
        first = 1 + 2 * layer

        for r in (1, 2, 7, 8) if layer == 0 else range(3, 7):
            conv_in(wa_in[layer], hid, r)
        for r in range(first + 1, 9 - first):
            row = (st[r] + conv_out(wa_out[layer], hid, r)).astype(BF16)
            if layer == 0:
                row = row.astype(F32) * jnp.where(valid(r), 1.0, 0.0)
                st[r] = row
                put_taps(r, row)
            else:
                arows.append(row[:, 0:384])

    flux = [
        jnp.dot(proj_ref[...], arows[i], preferred_element_type=F32).astype(BF16).astype(F32)
        for i in range(2)
    ]
    sub = [flux[b // 3][:, (b % 3) * 128 : (b % 3 + 1) * 128] for b in range(6)]
    weight_copies[2].wait()
    c_start, c_wait, c_done = swap(cs, cr, c_s, c_r)
    for i in range(nt):
        p = near_first(nt - 1 - i)
        out = []
        for s in range(2):
            source = jnp.full((8, 128), src_ref[s, p], jnp.int32)
            chosen = jnp.zeros((8, 128), F32)
            for b in range(6):
                chosen = jnp.where(source == b, sub[b], chosen)
            out.append(
                jnp.dot(
                    chosen.astype(BF16),
                    blk_v[wgt_ref[s, p]],
                    preferred_element_type=F32,
                )
            )
        cs[p] = jnp.concatenate(out, axis=0).astype(BF16)
        c_start(p)

    anext_ref[...] = jnp.stack([v.astype(F32) for v in arows], axis=1).astype(BF16)
    weight_copies[3].wait()
    stack_in(oin_v, wo_in)
    weight_copies[4].wait()
    wo_out[...] = jnp.zeros(wo_out.shape, BF16)
    stack_out(oout_v, wo_out, 40, 128)
    halos[1][1](NEAR + FAR)
    taps = [oin_v[0, tap].astype(F32)[40:48] for tap in range(9)]
    gap = [jnp.zeros((8, 128), F32)]
    wo_flux[...] = (
        jnp.concatenate(taps[0:3] + gap + taps[3:6] + gap + taps[6:9] + gap, axis=0).astype(BF16).T
    )
    for r in range(10):
        row = wide_row(1, r)
        st[r] = row
        put_taps(r, jnp.concatenate([row[0:40], jnp.zeros((8, WIDE), F32)], axis=0))

    def pre_in(r):
        patch = xp[r - 1 : r + 2].reshape(432, WIDE)
        pre[r - 1] = jnp.dot(wo_in[0], patch, preferred_element_type=F32)

    for r in range(1, 5):
        pre_in(r)
    for p in range(nt):
        tq_wait(p)

    total = [jnp.zeros((8, 128), F32) for b in range(6)]
    for p in range(nt):
        c_wait(p)
        arrived = cr[p].astype(F32)
        target = tq[p].astype(F32)
        for s in range(2):
            value, where_to = arrived[8 * s : 8 * s + 8], target[8 * s : 8 * s + 8]
            for b in range(6):
                total[b] = total[b] + jnp.where(where_to == b, value, 0.0)
    own = jnp.concatenate(
        [jnp.concatenate(total[0:3], axis=1), jnp.concatenate(total[3:6], axis=1)], axis=0
    )
    fmain[2] = own.astype(BF16)
    fedge_src[...] = jnp.where(lane < 64, own[:, 0:128], own[:, 256:384]).astype(BF16)
    f_start, f_wait, f_done = exchange(
        fmain.at[2], fmain, fedge_src, fedge, fms, fmr, fes, fer
    )
    f_start()
    for r in range(5, 9):
        pre_in(r)
    def flux_row(r):
        j, i = r // 2, r % 2
        got = [fedge[n, j].astype(F32) for n in range(len(sides))]
        side = got[0] if len(got) == 1 else jnp.where(lane < 64, got[1], got[0])
        both = jnp.concatenate([fmain[j].astype(F32), side], axis=1)
        return both[8 * i : 8 * i + 8]

    def flux_taps(rows):
        for r in rows:
            row = flux_row(r)
            xf[r] = jnp.concatenate(
                [
                    pltpu.roll(row, 1, 1),
                    row,
                    pltpu.roll(row, WIDE - 1, 1),
                    jnp.zeros((8, WIDE), F32),
                ],
                axis=0,
            ).astype(BF16)

    temp = None

    def flux_in(r):
        v = pre[r - 1] + jnp.dot(
            wo_flux[...], xf[r - 1 : r + 2].reshape(96, WIDE), preferred_element_type=F32
        )
        ohid[r - 1] = gelu(v, jnp.where(valid(r), 1.0, 0.0)).astype(BF16)
    for layer in range(2):
        first = 1 + 2 * layer

        if layer == 0:
            f_wait(NEAR)
            flux_taps(range(2, 8))
            loop(3, 7, flux_in)
            f_wait(FAR)
            flux_taps((0, 1, 8, 9))
            for r in (1, 2, 7, 8):
                flux_in(r)
        else:
            loop(first, 10 - first, lambda r: conv_in(wo_in[layer], ohid, r))
        rows = []
        for r in range(first + 1, 9 - first):
            y = conv_out(wo_out[layer], ohid, r)
            row = ((st[r, 0:40] + y[0:40]) * st[r, 40:41]).astype(BF16)
            if layer == 0:
                row = row.astype(F32) * jnp.where(valid(r), 1.0, 0.0)
                st[r, 0:40] = row
                put_taps(r, jnp.concatenate([row, flux_row(r)], axis=0))
            else:
                orows.append(row[:, 0:384])
                rows.append(row[0:16, 0:384].astype(F32)[0:1])
        temp = rows

    warm = [
        jnp.broadcast_to(temp[b // 3][:, (b % 3) * 128 : (b % 3 + 1) * 128], (16, 128))
        for b in range(6)
    ]
    b_start, b_wait, b_done = swap(bs, br, b_s, b_r)
    for i in range(nt):
        p = near_first(nt - 1 - i)
        target = tq[p].astype(F32)
        back = jnp.zeros((16, 128), F32)
        for b in range(6):
            back = jnp.where(target == b, warm[b], back)
        bs[p] = back.astype(BF16)
        b_start(p)
    onext_ref[...] = jnp.stack([v.astype(F32) for v in orows], axis=1).astype(BF16)
    heat = [jnp.zeros((8, 128), F32) for b in range(6)]
    for i in range(nt):
        p = near_first(i)
        b_wait(p)
        got = br[p].astype(F32)
        for s in range(2):
            piece = lax.dot_general(
                got[8 * s : 8 * s + 8].astype(BF16),
                blk_v[wgt_ref[s, p]],
                (((1,), (1,)), ((), ())),
                preferred_element_type=F32,
            )
            source = jnp.full((8, 128), src_ref[s, p], jnp.int32)
            for b in range(6):
                heat[b] = heat[b] + jnp.where(source == b, piece, 0.0)
    for b in range(6):
        temp_ref[b // 3 : b // 3 + 1, (b % 3) * 128 : (b % 3 + 1) * 128] = heat[b][0:1]

    halos[0][2]()
    halos[1][2]()
    tq_done()
    c_done()
    f_done()
    b_done()


def hand_out_kernel(*refs):
    sems = refs[6]
    copies = [
        pltpu.make_async_copy(source, target, sems.at[i])
        for i, (source, target) in enumerate(zip(refs[:3], refs[3:6]))
    ]
    for copy in copies:
        copy.start()
    for copy in copies:
        copy.wait()


def hand_out(*arrays):
    vmem = pl.BlockSpec(memory_space=pltpu.VMEM)
    return pl.pallas_call(
        hand_out_kernel,
        out_shape=tuple(jax.ShapeDtypeStruct(v.shape, v.dtype) for v in arrays),
        in_specs=[vmem] * 3,
        out_specs=(pl.BlockSpec(memory_space=pltpu.HBM),) * 3,
        scratch_shapes=[pltpu.SemaphoreType.DMA((3,))],
    )(*[pltpu.with_memory_space_constraint(v, pltpu.VMEM) for v in arrays])


def per_device(
    dims,
    atmos_state,
    ocean_state,
    ocean_mask,
    atmos_in_w,
    atmos_out_w,
    ocean_in_w,
    ocean_out_w,
    flux_proj,
    regrid_blocks,
    regrid_source_block,
    regrid_target_block,
    regrid_weight_block,
):
    nt, nc, nl = dims
    sides = 1 if nl == 2 else 2
    in_taps = [w.transpose(0, 1, 3, 2) for w in (atmos_in_w, ocean_in_w)]
    links = [
        v.reshape(nt, 2).T
        for v in (regrid_source_block, regrid_target_block, regrid_weight_block)
    ]
    vmem = pl.BlockSpec(memory_space=pltpu.VMEM)
    hbm = pl.BlockSpec(memory_space=pltpu.HBM)
    dma = pltpu.SemaphoreType.DMA
    anext, onext, temp = pl.pallas_call(
        functools.partial(kernel, dims),
        out_shape=(
            pltpu.VMEM((48, 2, 384), BF16),
            pltpu.VMEM((40, 2, 384), BF16),
            pltpu.VMEM((2, 384), F32),
        ),
        in_specs=[hbm] * 12,
        out_specs=(vmem, vmem, vmem),
        scratch_shapes=[
            pltpu.SMEM((2, nt), jnp.int32),
            pltpu.SMEM((2, nt), jnp.int32),
            pltpu.SMEM((2, nt), jnp.int32),
            pltpu.VMEM(atmos_state.shape, BF16),
            pltpu.VMEM(ocean_state.shape, BF16),
            pltpu.VMEM(ocean_mask.shape, jnp.int32),
            pltpu.VMEM(flux_proj.shape, BF16),
            pltpu.VMEM(in_taps[0].shape, BF16),
            pltpu.VMEM(atmos_out_w.shape, BF16),
            pltpu.VMEM(in_taps[1].shape, BF16),
            pltpu.VMEM(ocean_out_w.shape, BF16),
            pltpu.VMEM(regrid_blocks.shape, BF16),
            pltpu.VMEM((2, 256, 432), BF16),
            pltpu.VMEM((2, 144, 768), BF16),
            pltpu.VMEM((2, 128, 432), BF16),
            pltpu.VMEM((2, 144, 384), BF16),
            pltpu.VMEM((2, 5, 2, 48, 384), BF16),
            pltpu.VMEM((2, 16, 128), BF16),
            pltpu.VMEM((2, sides, 5, 16, 128), BF16),
            pltpu.VMEM((10, 144, WIDE), BF16),
            pltpu.VMEM((10, 32, WIDE), BF16),
            pltpu.VMEM((8, 128, WIDE), F32),
            pltpu.VMEM((128, 96), BF16),
            pltpu.VMEM((8, 256, WIDE), BF16),
            pltpu.VMEM((8, 128, WIDE), BF16),
            pltpu.VMEM((10, 48, WIDE), F32),
            pltpu.VMEM((5, 16, 384), BF16),
            pltpu.VMEM((16, 128), BF16),
            pltpu.VMEM((sides, 5, 16, 128), BF16),
            pltpu.VMEM((nt, 16, 128), BF16),
            pltpu.VMEM((nt, 16, 128), BF16),
            pltpu.VMEM((nt, 16, 128), BF16),
            pltpu.VMEM((nt, 16, 128), BF16),
            pltpu.VMEM((nt, 16, 128), BF16),
            pltpu.VMEM((nt, 16, 128), BF16),
            dma((5,)),
            dma((7,)),
            dma((2, 5)),
            dma((2, 5)),
            dma((2, sides, 5)),
            dma((2, sides, 5)),
            dma((5,)),
            dma((5,)),
            dma((sides, 5)),
            dma((sides, 5)),
            dma((nt,)),
            dma((nt,)),
            dma((nt,)),
            dma((nt,)),
            dma((nt,)),
            dma((nt,)),
        ],
        compiler_params=pltpu.CompilerParams(
            collective_id=0, has_side_effects=True, vmem_limit_bytes=60 * 1024 * 1024
        ),
    )(
        *links,
        atmos_state,
        ocean_state,
        ocean_mask,
        flux_proj,
        in_taps[0],
        atmos_out_w,
        in_taps[1],
        ocean_out_w,
        regrid_blocks,
    )
    return hand_out(anext, onext, temp)


def solution(mesh):
    dims = (mesh.shape["lat"] * mesh.shape["comp"], mesh.shape["comp"], mesh.shape["lon"])
    field = P(None, ("grp", "lat", "comp"), "lon")
    plane = P(("grp", "lat", "comp"), "lon")
    links = P(("grp", "lat", "comp"), "lon", None, None)
    in_specs = (field, field, plane) + (P(),) * 6 + (links,) * 3
    return jax.shard_map(
        functools.partial(per_device, dims),
        mesh=mesh,
        in_specs=in_specs,
        out_specs=(field, field, plane),
        check_vma=False,
    )
```

```python
import functools

import jax
import jax.numpy as jnp
from jax import lax
from jax.experimental import pallas as pl
from jax.experimental.pallas import tpu as pltpu
from jax.sharding import PartitionSpec as P

MESH = pl.DeviceIdType.MESH
F32 = jnp.float32
BF16 = jnp.bfloat16
WIDE = 512
NEAR = (0, 1, -1)
FAR = (2, -2)


def gelu(v, keep):
    v = v.astype(BF16)
    half = (0.5 * keep).astype(BF16) * v
    slope = jnp.asarray(0.7978845608 * 0.044715, BF16) * (v * v)
    return half + half * jnp.tanh(v * (jnp.asarray(0.7978845608, BF16) + slope))


def kernel(
    dims,
    src_hbm,
    tgt_hbm,
    wgt_hbm,
    atmos_hbm,
    ocean_hbm,
    mask_hbm,
    proj_hbm,
    ain_hbm,
    aout_hbm,
    oin_hbm,
    oout_hbm,
    blk_hbm,
    anext_ref,
    onext_ref,
    temp_ref,
    src_ref,
    tgt_ref,
    wgt_ref,
    atmos_ref,
    ocean_ref,
    mask_ref,
    proj_ref,
    ain_v,
    aout_v,
    oin_v,
    oout_v,
    blk_v,
    wa_in,
    wa_out,
    wo_in,
    wo_out,
    main,
    rim,
    edge,
    xp,
    xf,
    pre,
    wo_flux,
    hid,
    ohid,
    st,
    fmain,
    fedge_src,
    fedge,
    tq_src,
    tq,
    cs,
    cr,
    bs,
    br,
    w_sem,
    i_sem,
    ms,
    mr,
    es,
    er,
    fms,
    fmr,
    fes,
    fer,
    tqs,
    tqr,
    c_s,
    c_r,
    b_s,
    b_r,
):
    nt, nc, nl = dims
    comp = lax.axis_index("comp")
    lat = lax.axis_index("lat")
    lon = lax.axis_index("lon")
    t = lat * nc + comp
    sides = (1,) if nl == 2 else (1, nl - 1)

    def dev(tt, ll):
        return {"lat": lax.div(tt, nc), "comp": lax.rem(tt, nc), "lon": ll}

    upper = lax.div(t, nt // 2)

    def near_first(i):
        return i + upper * (nt - 1 - 2 * i)

    def inside(d):
        return (t + d >= 0) & (t + d < nt)

    barrier = pltpu.get_barrier_semaphore()
    for k in range(1, nt):
        pl.semaphore_signal(
            barrier, inc=1, device_id=dev(lax.rem(t + k, nt), lon), device_id_type=MESH
        )
    for e in range(-2, 3):

        @pl.when(inside(e))
        def _():
            for s in sides:
                pl.semaphore_signal(
                    barrier,
                    inc=1,
                    device_id=dev(t + e, lax.rem(lon + s, nl)),
                    device_id_type=MESH,
                )

    input_copies = [
        pltpu.make_async_copy(src, dst, i_sem.at[i])
        for i, (src, dst) in enumerate(
            (
                (atmos_hbm, atmos_ref),
                (tgt_hbm, tgt_ref),
                (ocean_hbm, ocean_ref),
                (mask_hbm, mask_ref),
                (src_hbm, src_ref),
                (wgt_hbm, wgt_ref),
                (proj_hbm, proj_ref),
            )
        )
    ]
    for copy in input_copies:
        copy.start()
    weight_copies = [
        pltpu.make_async_copy(src, dst, w_sem.at[i])
        for i, (src, dst) in enumerate(
            (
                (ain_hbm, ain_v),
                (aout_hbm, aout_v),
                (blk_hbm, blk_v),
                (oin_hbm, oin_v),
                (oout_hbm, oout_v),
            )
        )
    ]
    for copy in weight_copies:
        copy.start()
    lane = lax.broadcasted_iota(jnp.int32, (16, 128), 1)

    def own_rows(m, rows):
        for i in range(2):
            main[m, 2, i] = rows[i].astype(BF16)

    def own_rim(m, rows):
        packed = jnp.zeros((16, 128), F32)
        for i in range(2):
            for g in range(3):
                q = i * 3 + g
                part = rows[i][16 * g : 16 * g + 16]
                ends = jnp.where(lane < 64, part[:, 0:128], part[:, 256:384])
                moved = pltpu.roll(ends, 16 * q + 8, 1)
                packed = jnp.where((lane >= 16 * q) & (lane < 16 * q + 16), moved, packed)
        rim[m] = packed.astype(BF16)

    def exchange(main_src, main_dst, edge_src, edge_dst, msend, mrecv, esend, erecv):
        def main_copy(e, out):
            j = 2 - e if out else e + 2
            return pltpu.make_async_remote_copy(
                src_ref=main_src,
                dst_ref=main_dst.at[j],
                send_sem=msend.at[e + 2],
                recv_sem=mrecv.at[j],
                device_id=dev(t + e, lon),
                device_id_type=MESH,
            )

        def edge_copy(e, n, s, out):
            j = 2 - e if out else e + 2
            return pltpu.make_async_remote_copy(
                src_ref=edge_src,
                dst_ref=edge_dst.at[n, j],
                send_sem=esend.at[n, e + 2],
                recv_sem=erecv.at[n, j],
                device_id=dev(t + e, lax.rem(lon + s, nl)),
                device_id_type=MESH,
            )

        def start():
            for places in ((-1, 1, 0), (-2, 2)):
                for e in places:

                    @pl.when(inside(e))
                    def _():
                        for n, s in enumerate(sides):
                            edge_copy(e, n, s, True).start()

                for e in places:
                    if e != 0:

                        @pl.when(inside(e))
                        def _():
                            main_copy(e, True).start()

        def wait_recv(places):
            for d in places:

                @pl.when(inside(d))
                def _():
                    for n, s in enumerate(sides):
                        edge_copy(d, n, s, False).wait_recv()
                    if d != 0:
                        main_copy(d, False).wait_recv()

                if d != 0:

                    @pl.when(jnp.logical_not(inside(d)))
                    def _():
                        main_dst[d + 2] = jnp.zeros(main_dst.shape[1:], main_dst.dtype)
                        for n in range(len(sides)):
                            edge_dst[n, d + 2] = jnp.zeros(edge_dst.shape[2:], edge_dst.dtype)

        def wait_send():
            for e in (-2, 2, -1, 1, 0):

                @pl.when(inside(e))
                def _():
                    if e != 0:
                        main_copy(e, True).wait_send()
                    for n, s in enumerate(sides):
                        edge_copy(e, n, s, True).wait_send()

        return start, wait_recv, wait_send

    def swap(src, dst, ssem, rsem):
        def copy(p, out):
            return pltpu.make_async_remote_copy(
                src_ref=src.at[p],
                dst_ref=dst.at[t if out else p],
                send_sem=ssem.at[p],
                recv_sem=rsem.at[t if out else p],
                device_id=dev(jnp.int32(p), lon),
                device_id_type=MESH,
            )

        def start(p):
            @pl.when(t != p)
            def _():
                copy(p, True).start()

            @pl.when(t == p)
            def _():
                dst[p] = src[p]

        def wait_recv(p):
            @pl.when(t != p)
            def _():
                copy(p, False).wait_recv()

        def wait_send():
            for p in range(nt):

                @pl.when(t != p)
                def _():
                    copy(p, True).wait_send()

        return start, wait_recv, wait_send

    halos = [
        exchange(
            main.at[m, 2],
            main.at[m],
            rim.at[m],
            edge.at[m],
            ms.at[m],
            mr.at[m],
            es.at[m],
            er.at[m],
        )
        for m in range(2)
    ]
    input_copies[0].wait()
    atmos_rows = [atmos_ref[:, i, :].astype(F32) for i in range(2)]
    own_rows(0, atmos_rows)
    own_rim(0, atmos_rows)
    low = jnp.minimum(t, 2)
    high = jnp.minimum(nt - 1 - t, 2)
    pl.semaphore_wait(barrier, nt - 1 + len(sides) * (low + high + 1))
    halos[0][0]()
    input_copies[1].wait()
    for p in range(nt):
        tq_src[p] = jnp.concatenate(
            [jnp.full((8, 128), tgt_ref[s, p], jnp.int32) for s in range(2)], axis=0
        ).astype(F32).astype(BF16)
    for copy in input_copies[2:]:
        copy.wait()
    wet = mask_ref[...].astype(F32)
    ocean_rows = [
        jnp.concatenate(
            [
                ocean_ref[:, i, :].astype(F32) * wet[i : i + 1],
                jnp.broadcast_to(wet[i : i + 1], (8, 384)),
            ],
            axis=0,
        )
        for i in range(2)
    ]
    own_rows(1, ocean_rows)
    own_rim(1, ocean_rows)
    tq_start, tq_wait, tq_done = swap(tq_src, tq, tqs, tqr)

    def stack_in(src, dst):
        for k in range(2):
            dst[k] = src[k].reshape(432, src.shape[3]).T

    def stack_out(src, dst, c, h):
        for k in range(2):
            for a in range(3):
                for b in range(3):
                    dst[k, b * 48 : b * 48 + c, a * h : (a + 1) * h] = src[k, 3 * a + b]

    weight_copies[0].wait()
    stack_in(ain_v, wa_in)
    weight_copies[1].wait()
    stack_out(aout_v, wa_out, 48, 256)

    def valid(r):
        row = 2 * t + r - 4
        return (row >= 0) & (row < 2 * nt)

    def wide_row(m, r):
        j, i = r // 2, r % 2
        pieces = []
        for g in range(3):
            shift = (120 - (i * 3 + g) * 16) % 128
            got = [pltpu.roll(edge[m, n, j].astype(F32), shift, 1) for n in range(len(sides))]
            pieces.append(got[0] if len(got) == 1 else jnp.where(lane < 64, got[1], got[0]))
        return jnp.concatenate(
            [main[m, j, i].astype(F32), jnp.concatenate(pieces, axis=0)], axis=1
        )

    def put_taps(r, row):
        row = row.astype(BF16)
        xp[r, 0:48] = pltpu.roll(row, 1, 1)
        xp[r, 48:96] = row
        xp[r, 96:144] = pltpu.roll(row, WIDE - 1, 1)

    def conv_in(w, buf, r):
        patch = xp[pl.ds(r - 1, 3)].reshape(432, WIDE)
        v = jnp.dot(w, patch, preferred_element_type=F32)
        buf[r - 1] = gelu(v, jnp.where(valid(r), 1.0, 0.0)).astype(BF16)

    def conv_out(w, buf, r):
        h = buf.shape[1]
        y = jnp.dot(w, buf[pl.ds(r - 2, 3)].reshape(3 * h, WIDE), preferred_element_type=F32)
        return pltpu.roll(y[0:48], 1, 1) + y[48:96] + pltpu.roll(y[96:144], WIDE - 1, 1)

    def loop(lo, hi, fn):
        for r in range(lo, hi):
            fn(r)

    def load_rows(rows):
        for r in rows:
            row = wide_row(0, r)
            put_taps(r, row)
            if 2 <= r < 8:
                st[r] = row

    halos[0][1](NEAR)
    load_rows(range(2, 8))
    loop(3, 7, lambda r: conv_in(wa_in[0], hid, r))
    halos[1][0]()
    halos[0][1](FAR)
    for i in range(nt):
        tq_start(near_first(i))
    load_rows((0, 1, 8, 9))

    arows, orows = [], []
    for layer in range(2):
        first = 1 + 2 * layer

        for r in (1, 2, 7, 8) if layer == 0 else range(3, 7):
            conv_in(wa_in[layer], hid, r)
        for r in range(first + 1, 9 - first):
            row = (st[r] + conv_out(wa_out[layer], hid, r)).astype(BF16)
            if layer == 0:
                row = row.astype(F32) * jnp.where(valid(r), 1.0, 0.0)
                st[r] = row
                put_taps(r, row)
            else:
                arows.append(row[:, 0:384])

    flux = [
        jnp.dot(proj_ref[...], arows[i], preferred_element_type=F32).astype(BF16).astype(F32)
        for i in range(2)
    ]
    sub = [flux[b // 3][:, (b % 3) * 128 : (b % 3 + 1) * 128] for b in range(6)]
    weight_copies[2].wait()
    c_start, c_wait, c_done = swap(cs, cr, c_s, c_r)
    for i in range(nt):
        p = near_first(nt - 1 - i)
        out = []
        for s in range(2):
            source = jnp.full((8, 128), src_ref[s, p], jnp.int32)
            chosen = jnp.zeros((8, 128), F32)
            for b in range(6):
                chosen = jnp.where(source == b, sub[b], chosen)
            out.append(
                jnp.dot(
                    chosen.astype(BF16),
                    blk_v[wgt_ref[s, p]],
                    preferred_element_type=F32,
                )
            )
        cs[p] = jnp.concatenate(out, axis=0).astype(BF16)
        c_start(p)

    anext_ref[...] = jnp.stack([v.astype(F32) for v in arows], axis=1).astype(BF16)
    weight_copies[3].wait()
    stack_in(oin_v, wo_in)
    weight_copies[4].wait()
    wo_out[...] = jnp.zeros(wo_out.shape, BF16)
    stack_out(oout_v, wo_out, 40, 128)
    halos[1][1](NEAR + FAR)
    taps = [oin_v[0, tap].astype(F32)[40:48] for tap in range(9)]
    gap = [jnp.zeros((8, 128), F32)]
    wo_flux[...] = (
        jnp.concatenate(taps[0:3] + gap + taps[3:6] + gap + taps[6:9] + gap, axis=0).astype(BF16).T
    )
    for r in range(10):
        row = wide_row(1, r)
        st[r] = row
        put_taps(r, jnp.concatenate([row[0:40], jnp.zeros((8, WIDE), F32)], axis=0))

    def pre_in(r):
        patch = xp[r - 1 : r + 2].reshape(432, WIDE)
        pre[r - 1] = jnp.dot(wo_in[0], patch, preferred_element_type=F32)

    for r in range(1, 5):
        pre_in(r)
    for p in range(nt):
        tq_wait(p)

    total = [jnp.zeros((8, 128), F32) for b in range(6)]
    for i in range(nt):
        p = near_first(i)
        c_wait(p)
        arrived = cr[p].astype(F32)
        target = tq[p].astype(F32)
        for s in range(2):
            value, where_to = arrived[8 * s : 8 * s + 8], target[8 * s : 8 * s + 8]
            for b in range(6):
                total[b] = total[b] + jnp.where(where_to == b, value, 0.0)
    own = jnp.concatenate(
        [jnp.concatenate(total[0:3], axis=1), jnp.concatenate(total[3:6], axis=1)], axis=0
    )
    fmain[2] = own.astype(BF16)
    fedge_src[...] = jnp.where(lane < 64, own[:, 0:128], own[:, 256:384]).astype(BF16)
    f_start, f_wait, f_done = exchange(
        fmain.at[2], fmain, fedge_src, fedge, fms, fmr, fes, fer
    )
    f_start()
    for r in range(5, 9):
        pre_in(r)
    def flux_row(r):
        j, i = r // 2, r % 2
        got = [fedge[n, j].astype(F32) for n in range(len(sides))]
        side = got[0] if len(got) == 1 else jnp.where(lane < 64, got[1], got[0])
        both = jnp.concatenate([fmain[j].astype(F32), side], axis=1)
        return both[8 * i : 8 * i + 8]

    def flux_taps(rows):
        for r in rows:
            row = flux_row(r)
            xf[r] = jnp.concatenate(
                [
                    pltpu.roll(row, 1, 1),
                    row,
                    pltpu.roll(row, WIDE - 1, 1),
                    jnp.zeros((8, WIDE), F32),
                ],
                axis=0,
            ).astype(BF16)

    temp = None

    def flux_in(r):
        v = pre[r - 1] + jnp.dot(
            wo_flux[...], xf[r - 1 : r + 2].reshape(96, WIDE), preferred_element_type=F32
        )
        ohid[r - 1] = gelu(v, jnp.where(valid(r), 1.0, 0.0)).astype(BF16)
    for layer in range(2):
        first = 1 + 2 * layer

        if layer == 0:
            f_wait(NEAR)
            flux_taps(range(2, 8))
            loop(3, 7, flux_in)
            f_wait(FAR)
            flux_taps((0, 1, 8, 9))
            for r in (1, 2, 7, 8):
                flux_in(r)
        else:
            loop(first, 10 - first, lambda r: conv_in(wo_in[layer], ohid, r))
        rows = []
        for r in range(first + 1, 9 - first):
            y = conv_out(wo_out[layer], ohid, r)
            row = ((st[r, 0:40] + y[0:40]) * st[r, 40:41]).astype(BF16)
            if layer == 0:
                row = row.astype(F32) * jnp.where(valid(r), 1.0, 0.0)
                st[r, 0:40] = row
                put_taps(r, jnp.concatenate([row, flux_row(r)], axis=0))
            else:
                orows.append(row[:, 0:384])
                rows.append(row[0:16, 0:384].astype(F32)[0:1])
        temp = rows

    warm = [
        jnp.broadcast_to(temp[b // 3][:, (b % 3) * 128 : (b % 3 + 1) * 128], (16, 128))
        for b in range(6)
    ]
    b_start, b_wait, b_done = swap(bs, br, b_s, b_r)
    for i in range(nt):
        p = near_first(nt - 1 - i)
        target = tq[p].astype(F32)
        back = jnp.zeros((16, 128), F32)
        for b in range(6):
            back = jnp.where(target == b, warm[b], back)
        bs[p] = back.astype(BF16)
        b_start(p)
    onext_ref[...] = jnp.stack([v.astype(F32) for v in orows], axis=1).astype(BF16)
    heat = [jnp.zeros((8, 128), F32) for b in range(6)]
    for i in range(nt):
        p = near_first(i)
        b_wait(p)
        got = br[p].astype(F32)
        for s in range(2):
            piece = lax.dot_general(
                got[8 * s : 8 * s + 8].astype(BF16),
                blk_v[wgt_ref[s, p]],
                (((1,), (1,)), ((), ())),
                preferred_element_type=F32,
            )
            source = jnp.full((8, 128), src_ref[s, p], jnp.int32)
            for b in range(6):
                heat[b] = heat[b] + jnp.where(source == b, piece, 0.0)
    for b in range(6):
        temp_ref[b // 3 : b // 3 + 1, (b % 3) * 128 : (b % 3 + 1) * 128] = heat[b][0:1]

    halos[0][2]()
    halos[1][2]()
    tq_done()
    c_done()
    f_done()
    b_done()


def hand_out_kernel(*refs):
    sems = refs[6]
    copies = [
        pltpu.make_async_copy(source, target, sems.at[i])
        for i, (source, target) in enumerate(zip(refs[:3], refs[3:6]))
    ]
    for copy in copies:
        copy.start()
    for copy in copies:
        copy.wait()


def hand_out(*arrays):
    vmem = pl.BlockSpec(memory_space=pltpu.VMEM)
    return pl.pallas_call(
        hand_out_kernel,
        out_shape=tuple(jax.ShapeDtypeStruct(v.shape, v.dtype) for v in arrays),
        in_specs=[vmem] * 3,
        out_specs=(pl.BlockSpec(memory_space=pltpu.HBM),) * 3,
        scratch_shapes=[pltpu.SemaphoreType.DMA((3,))],
    )(*[pltpu.with_memory_space_constraint(v, pltpu.VMEM) for v in arrays])


def per_device(
    dims,
    atmos_state,
    ocean_state,
    ocean_mask,
    atmos_in_w,
    atmos_out_w,
    ocean_in_w,
    ocean_out_w,
    flux_proj,
    regrid_blocks,
    regrid_source_block,
    regrid_target_block,
    regrid_weight_block,
):
    nt, nc, nl = dims
    sides = 1 if nl == 2 else 2
    in_taps = [w.transpose(0, 1, 3, 2) for w in (atmos_in_w, ocean_in_w)]
    links = [
        v.reshape(nt, 2).T
        for v in (regrid_source_block, regrid_target_block, regrid_weight_block)
    ]
    vmem = pl.BlockSpec(memory_space=pltpu.VMEM)
    hbm = pl.BlockSpec(memory_space=pltpu.HBM)
    dma = pltpu.SemaphoreType.DMA
    anext, onext, temp = pl.pallas_call(
        functools.partial(kernel, dims),
        out_shape=(
            pltpu.VMEM((48, 2, 384), BF16),
            pltpu.VMEM((40, 2, 384), BF16),
            pltpu.VMEM((2, 384), F32),
        ),
        in_specs=[hbm] * 12,
        out_specs=(vmem, vmem, vmem),
        scratch_shapes=[
            pltpu.SMEM((2, nt), jnp.int32),
            pltpu.SMEM((2, nt), jnp.int32),
            pltpu.SMEM((2, nt), jnp.int32),
            pltpu.VMEM(atmos_state.shape, BF16),
            pltpu.VMEM(ocean_state.shape, BF16),
            pltpu.VMEM(ocean_mask.shape, jnp.int32),
            pltpu.VMEM(flux_proj.shape, BF16),
            pltpu.VMEM(in_taps[0].shape, BF16),
            pltpu.VMEM(atmos_out_w.shape, BF16),
            pltpu.VMEM(in_taps[1].shape, BF16),
            pltpu.VMEM(ocean_out_w.shape, BF16),
            pltpu.VMEM(regrid_blocks.shape, BF16),
            pltpu.VMEM((2, 256, 432), BF16),
            pltpu.VMEM((2, 144, 768), BF16),
            pltpu.VMEM((2, 128, 432), BF16),
            pltpu.VMEM((2, 144, 384), BF16),
            pltpu.VMEM((2, 5, 2, 48, 384), BF16),
            pltpu.VMEM((2, 16, 128), BF16),
            pltpu.VMEM((2, sides, 5, 16, 128), BF16),
            pltpu.VMEM((10, 144, WIDE), BF16),
            pltpu.VMEM((10, 32, WIDE), BF16),
            pltpu.VMEM((8, 128, WIDE), F32),
            pltpu.VMEM((128, 96), BF16),
            pltpu.VMEM((8, 256, WIDE), BF16),
            pltpu.VMEM((8, 128, WIDE), BF16),
            pltpu.VMEM((10, 48, WIDE), F32),
            pltpu.VMEM((5, 16, 384), BF16),
            pltpu.VMEM((16, 128), BF16),
            pltpu.VMEM((sides, 5, 16, 128), BF16),
            pltpu.VMEM((nt, 16, 128), BF16),
            pltpu.VMEM((nt, 16, 128), BF16),
            pltpu.VMEM((nt, 16, 128), BF16),
            pltpu.VMEM((nt, 16, 128), BF16),
            pltpu.VMEM((nt, 16, 128), BF16),
            pltpu.VMEM((nt, 16, 128), BF16),
            dma((5,)),
            dma((7,)),
            dma((2, 5)),
            dma((2, 5)),
            dma((2, sides, 5)),
            dma((2, sides, 5)),
            dma((5,)),
            dma((5,)),
            dma((sides, 5)),
            dma((sides, 5)),
            dma((nt,)),
            dma((nt,)),
            dma((nt,)),
            dma((nt,)),
            dma((nt,)),
            dma((nt,)),
        ],
        compiler_params=pltpu.CompilerParams(
            collective_id=0, has_side_effects=True, vmem_limit_bytes=60 * 1024 * 1024
        ),
    )(
        *links,
        atmos_state,
        ocean_state,
        ocean_mask,
        flux_proj,
        in_taps[0],
        atmos_out_w,
        in_taps[1],
        ocean_out_w,
        regrid_blocks,
    )
    return hand_out(anext, onext, temp)


def solution(mesh):
    dims = (mesh.shape["lat"] * mesh.shape["comp"], mesh.shape["comp"], mesh.shape["lon"])
    field = P(None, ("grp", "lat", "comp"), "lon")
    plane = P(("grp", "lat", "comp"), "lon")
    links = P(("grp", "lat", "comp"), "lon", None, None)
    in_specs = (field, field, plane) + (P(),) * 6 + (links,) * 3
    return jax.shard_map(
        functools.partial(per_device, dims),
        mesh=mesh,
        in_specs=in_specs,
        out_specs=(field, field, plane),
        check_vma=False,
    )
```

```python
import functools

import jax
import jax.numpy as jnp
from jax import lax
from jax.experimental import pallas as pl
from jax.experimental.pallas import tpu as pltpu
from jax.sharding import PartitionSpec as P

MESH = pl.DeviceIdType.MESH
F32 = jnp.float32
BF16 = jnp.bfloat16
WIDE = 512
NEAR = (0, 1, -1)
FAR = (2, -2)


def gelu(v, keep):
    v = v.astype(BF16)
    half = (0.5 * keep).astype(BF16) * v
    slope = jnp.asarray(0.7978845608 * 0.044715, BF16) * (v * v)
    return half + half * jnp.tanh(v * (jnp.asarray(0.7978845608, BF16) + slope))


def kernel(
    dims,
    src_hbm,
    tgt_hbm,
    wgt_hbm,
    atmos_hbm,
    ocean_hbm,
    mask_hbm,
    proj_hbm,
    ain_hbm,
    aout_hbm,
    oin_hbm,
    oout_hbm,
    blk_hbm,
    anext_ref,
    onext_ref,
    temp_ref,
    src_ref,
    tgt_ref,
    wgt_ref,
    atmos_ref,
    ocean_ref,
    mask_ref,
    proj_ref,
    ain_v,
    aout_v,
    oin_v,
    oout_v,
    blk_v,
    wa_in,
    wa_out,
    wo_in,
    wo_out,
    main,
    rim,
    edge,
    xp,
    xf,
    pre,
    wo_flux,
    hid,
    ohid,
    st,
    fmain,
    fedge_src,
    fedge,
    tq_src,
    tq,
    cs,
    cr,
    bs,
    br,
    w_sem,
    i_sem,
    ms,
    mr,
    es,
    er,
    fms,
    fmr,
    fes,
    fer,
    tqs,
    tqr,
    c_s,
    c_r,
    b_s,
    b_r,
):
    nt, nc, nl = dims
    comp = lax.axis_index("comp")
    lat = lax.axis_index("lat")
    lon = lax.axis_index("lon")
    t = lat * nc + comp
    sides = (1,) if nl == 2 else (1, nl - 1)

    def dev(tt, ll):
        return {"lat": lax.div(tt, nc), "comp": lax.rem(tt, nc), "lon": ll}

    upper = lax.div(t, nt // 2)

    def near_first(i):
        return i + upper * (nt - 1 - 2 * i)

    place = near_first(t)

    def peer(i):
        return near_first(i + lax.div(i + nt - place, nt))

    peers = [peer(i) for i in range(nt - 1)]

    def inside(d):
        return (t + d >= 0) & (t + d < nt)

    barrier = pltpu.get_barrier_semaphore()
    for k in range(1, nt):
        pl.semaphore_signal(
            barrier, inc=1, device_id=dev(lax.rem(t + k, nt), lon), device_id_type=MESH
        )
    for e in range(-2, 3):

        @pl.when(inside(e))
        def _():
            for s in sides:
                pl.semaphore_signal(
                    barrier,
                    inc=1,
                    device_id=dev(t + e, lax.rem(lon + s, nl)),
                    device_id_type=MESH,
                )

    input_copies = [
        pltpu.make_async_copy(src, dst, i_sem.at[i])
        for i, (src, dst) in enumerate(
            (
                (atmos_hbm, atmos_ref),
                (tgt_hbm, tgt_ref),
                (ocean_hbm, ocean_ref),
                (mask_hbm, mask_ref),
                (src_hbm, src_ref),
                (wgt_hbm, wgt_ref),
                (proj_hbm, proj_ref),
            )
        )
    ]
    for copy in input_copies:
        copy.start()
    weight_copies = [
        pltpu.make_async_copy(src, dst, w_sem.at[i])
        for i, (src, dst) in enumerate(
            (
                (ain_hbm, ain_v),
                (aout_hbm, aout_v),
                (blk_hbm, blk_v),
                (oin_hbm, oin_v),
                (oout_hbm, oout_v),
            )
        )
    ]
    for copy in weight_copies:
        copy.start()
    lane = lax.broadcasted_iota(jnp.int32, (16, 128), 1)

    def own_rows(m, rows):
        for i in range(2):
            main[m, 2, i] = rows[i].astype(BF16)

    def own_rim(m, rows):
        packed = jnp.zeros((16, 128), F32)
        for i in range(2):
            for g in range(3):
                q = i * 3 + g
                part = rows[i][16 * g : 16 * g + 16]
                ends = jnp.where(lane < 64, part[:, 0:128], part[:, 256:384])
                moved = pltpu.roll(ends, 16 * q + 8, 1)
                packed = jnp.where((lane >= 16 * q) & (lane < 16 * q + 16), moved, packed)
        rim[m] = packed.astype(BF16)

    def exchange(main_src, main_dst, edge_src, edge_dst, msend, mrecv, esend, erecv):
        def main_copy(e, out):
            j = 2 - e if out else e + 2
            return pltpu.make_async_remote_copy(
                src_ref=main_src,
                dst_ref=main_dst.at[j],
                send_sem=msend.at[e + 2],
                recv_sem=mrecv.at[j],
                device_id=dev(t + e, lon),
                device_id_type=MESH,
            )

        def edge_copy(e, n, s, out):
            j = 2 - e if out else e + 2
            return pltpu.make_async_remote_copy(
                src_ref=edge_src,
                dst_ref=edge_dst.at[n, j],
                send_sem=esend.at[n, e + 2],
                recv_sem=erecv.at[n, j],
                device_id=dev(t + e, lax.rem(lon + s, nl)),
                device_id_type=MESH,
            )

        def start():
            for places in ((-1, 1, 0), (-2, 2)):
                for e in places:

                    @pl.when(inside(e))
                    def _():
                        for n, s in enumerate(sides):
                            edge_copy(e, n, s, True).start()

                for e in places:
                    if e != 0:

                        @pl.when(inside(e))
                        def _():
                            main_copy(e, True).start()

        def wait_recv(places):
            for d in places:

                @pl.when(inside(d))
                def _():
                    for n, s in enumerate(sides):
                        edge_copy(d, n, s, False).wait_recv()
                    if d != 0:
                        main_copy(d, False).wait_recv()

                if d != 0:

                    @pl.when(jnp.logical_not(inside(d)))
                    def _():
                        main_dst[d + 2] = jnp.zeros(main_dst.shape[1:], main_dst.dtype)
                        for n in range(len(sides)):
                            edge_dst[n, d + 2] = jnp.zeros(edge_dst.shape[2:], edge_dst.dtype)

        def wait_send():
            for e in (-2, 2, -1, 1, 0):

                @pl.when(inside(e))
                def _():
                    if e != 0:
                        main_copy(e, True).wait_send()
                    for n, s in enumerate(sides):
                        edge_copy(e, n, s, True).wait_send()

        return start, wait_recv, wait_send

    def swap(src, dst, ssem, rsem):
        def copy(p, out):
            return pltpu.make_async_remote_copy(
                src_ref=src.at[p],
                dst_ref=dst.at[t if out else p],
                send_sem=ssem.at[p],
                recv_sem=rsem.at[t if out else p],
                device_id=dev(p, lon),
                device_id_type=MESH,
            )

        def start():
            for p in reversed(peers):
                copy(p, True).start()
            dst[t] = src[t]

        def wait_recv(p):
            copy(p, False).wait_recv()

        def wait_send():
            for p in peers:
                copy(p, True).wait_send()

        return start, wait_recv, wait_send

    halos = [
        exchange(
            main.at[m, 2],
            main.at[m],
            rim.at[m],
            edge.at[m],
            ms.at[m],
            mr.at[m],
            es.at[m],
            er.at[m],
        )
        for m in range(2)
    ]
    input_copies[0].wait()
    atmos_rows = [atmos_ref[:, i, :].astype(F32) for i in range(2)]
    own_rows(0, atmos_rows)
    own_rim(0, atmos_rows)
    low = jnp.minimum(t, 2)
    high = jnp.minimum(nt - 1 - t, 2)
    pl.semaphore_wait(barrier, nt - 1 + len(sides) * (low + high + 1))
    halos[0][0]()
    input_copies[1].wait()
    for p in range(nt):
        tq_src[p] = jnp.concatenate(
            [jnp.full((8, 128), tgt_ref[s, p], jnp.int32) for s in range(2)], axis=0
        ).astype(F32).astype(BF16)
    for copy in input_copies[2:]:
        copy.wait()
    wet = mask_ref[...].astype(F32)
    ocean_rows = [
        jnp.concatenate(
            [
                ocean_ref[:, i, :].astype(F32) * wet[i : i + 1],
                jnp.broadcast_to(wet[i : i + 1], (8, 384)),
            ],
            axis=0,
        )
        for i in range(2)
    ]
    own_rows(1, ocean_rows)
    own_rim(1, ocean_rows)
    tq_start, tq_wait, tq_done = swap(tq_src, tq, tqs, tqr)

    def stack_in(src, dst):
        for k in range(2):
            dst[k] = src[k].reshape(432, src.shape[3]).T

    def stack_out(src, dst, c, h):
        for k in range(2):
            for a in range(3):
                for b in range(3):
                    dst[k, b * 48 : b * 48 + c, a * h : (a + 1) * h] = src[k, 3 * a + b]

    weight_copies[0].wait()
    stack_in(ain_v, wa_in)
    weight_copies[1].wait()
    stack_out(aout_v, wa_out, 48, 256)

    def valid(r):
        row = 2 * t + r - 4
        return (row >= 0) & (row < 2 * nt)

    def wide_row(m, r):
        j, i = r // 2, r % 2
        pieces = []
        for g in range(3):
            shift = (120 - (i * 3 + g) * 16) % 128
            got = [pltpu.roll(edge[m, n, j].astype(F32), shift, 1) for n in range(len(sides))]
            pieces.append(got[0] if len(got) == 1 else jnp.where(lane < 64, got[1], got[0]))
        return jnp.concatenate(
            [main[m, j, i].astype(F32), jnp.concatenate(pieces, axis=0)], axis=1
        )

    def put_taps(r, row):
        row = row.astype(BF16)
        xp[r, 0:48] = pltpu.roll(row, 1, 1)
        xp[r, 48:96] = row
        xp[r, 96:144] = pltpu.roll(row, WIDE - 1, 1)

    def conv_in(w, buf, r):
        patch = xp[pl.ds(r - 1, 3)].reshape(432, WIDE)
        v = jnp.dot(w, patch, preferred_element_type=F32)
        buf[r - 1] = gelu(v, jnp.where(valid(r), 1.0, 0.0)).astype(BF16)

    def conv_out(w, buf, r):
        h = buf.shape[1]
        y = jnp.dot(w, buf[pl.ds(r - 2, 3)].reshape(3 * h, WIDE), preferred_element_type=F32)
        return pltpu.roll(y[0:48], 1, 1) + y[48:96] + pltpu.roll(y[96:144], WIDE - 1, 1)

    def loop(lo, hi, fn):
        for r in range(lo, hi):
            fn(r)

    def load_rows(rows):
        for r in rows:
            row = wide_row(0, r)
            put_taps(r, row)
            if 2 <= r < 8:
                st[r] = row

    halos[0][1](NEAR)
    load_rows(range(2, 8))
    loop(3, 7, lambda r: conv_in(wa_in[0], hid, r))
    halos[1][0]()
    halos[0][1](FAR)
    tq_start()
    load_rows((0, 1, 8, 9))

    arows, orows = [], []
    for layer in range(2):
        first = 1 + 2 * layer

        for r in (1, 2, 7, 8) if layer == 0 else range(3, 7):
            conv_in(wa_in[layer], hid, r)
        for r in range(first + 1, 9 - first):
            row = (st[r] + conv_out(wa_out[layer], hid, r)).astype(BF16)
            if layer == 0:
                row = row.astype(F32) * jnp.where(valid(r), 1.0, 0.0)
                st[r] = row
                put_taps(r, row)
            else:
                arows.append(row[:, 0:384])

    flux = [
        jnp.dot(proj_ref[...], arows[i], preferred_element_type=F32).astype(BF16).astype(F32)
        for i in range(2)
    ]
    sub = [flux[b // 3][:, (b % 3) * 128 : (b % 3 + 1) * 128] for b in range(6)]
    weight_copies[2].wait()
    c_start, c_wait, c_done = swap(cs, cr, c_s, c_r)
    for p in range(nt):
        out = []
        for s in range(2):
            source = jnp.full((8, 128), src_ref[s, p], jnp.int32)
            chosen = jnp.zeros((8, 128), F32)
            for b in range(6):
                chosen = jnp.where(source == b, sub[b], chosen)
            out.append(
                jnp.dot(
                    chosen.astype(BF16),
                    blk_v[wgt_ref[s, p]],
                    preferred_element_type=F32,
                )
            )
        cs[p] = jnp.concatenate(out, axis=0).astype(BF16)
    c_start()

    anext_ref[...] = jnp.stack([v.astype(F32) for v in arows], axis=1).astype(BF16)
    weight_copies[3].wait()
    stack_in(oin_v, wo_in)
    weight_copies[4].wait()
    wo_out[...] = jnp.zeros(wo_out.shape, BF16)
    stack_out(oout_v, wo_out, 40, 128)
    halos[1][1](NEAR + FAR)
    taps = [oin_v[0, tap].astype(F32)[40:48] for tap in range(9)]
    gap = [jnp.zeros((8, 128), F32)]
    wo_flux[...] = (
        jnp.concatenate(taps[0:3] + gap + taps[3:6] + gap + taps[6:9] + gap, axis=0).astype(BF16).T
    )
    for r in range(10):
        row = wide_row(1, r)
        st[r] = row
        put_taps(r, jnp.concatenate([row[0:40], jnp.zeros((8, WIDE), F32)], axis=0))

    def pre_in(r):
        patch = xp[r - 1 : r + 2].reshape(432, WIDE)
        pre[r - 1] = jnp.dot(wo_in[0], patch, preferred_element_type=F32)

    for r in range(1, 5):
        pre_in(r)
    for p in peers:
        tq_wait(p)

    total = [jnp.zeros((8, 128), F32) for b in range(6)]
    for p in [t] + peers:
        if p is not t:
            c_wait(p)
        arrived = cr[p].astype(F32)
        target = tq[p].astype(F32)
        for s in range(2):
            value, where_to = arrived[8 * s : 8 * s + 8], target[8 * s : 8 * s + 8]
            for b in range(6):
                total[b] = total[b] + jnp.where(where_to == b, value, 0.0)
    own = jnp.concatenate(
        [jnp.concatenate(total[0:3], axis=1), jnp.concatenate(total[3:6], axis=1)], axis=0
    )
    fmain[2] = own.astype(BF16)
    fedge_src[...] = jnp.where(lane < 64, own[:, 0:128], own[:, 256:384]).astype(BF16)
    f_start, f_wait, f_done = exchange(
        fmain.at[2], fmain, fedge_src, fedge, fms, fmr, fes, fer
    )
    f_start()
    for r in range(5, 9):
        pre_in(r)
    def flux_row(r):
        j, i = r // 2, r % 2
        got = [fedge[n, j].astype(F32) for n in range(len(sides))]
        side = got[0] if len(got) == 1 else jnp.where(lane < 64, got[1], got[0])
        both = jnp.concatenate([fmain[j].astype(F32), side], axis=1)
        return both[8 * i : 8 * i + 8]

    def flux_taps(rows):
        for r in rows:
            row = flux_row(r)
            xf[r] = jnp.concatenate(
                [
                    pltpu.roll(row, 1, 1),
                    row,
                    pltpu.roll(row, WIDE - 1, 1),
                    jnp.zeros((8, WIDE), F32),
                ],
                axis=0,
            ).astype(BF16)

    temp = None

    def flux_in(r):
        v = pre[r - 1] + jnp.dot(
            wo_flux[...], xf[r - 1 : r + 2].reshape(96, WIDE), preferred_element_type=F32
        )
        ohid[r - 1] = gelu(v, jnp.where(valid(r), 1.0, 0.0)).astype(BF16)
    for layer in range(2):
        first = 1 + 2 * layer

        if layer == 0:
            f_wait(NEAR)
            flux_taps(range(2, 8))
            loop(3, 7, flux_in)
            f_wait(FAR)
            flux_taps((0, 1, 8, 9))
            for r in (1, 2, 7, 8):
                flux_in(r)
        else:
            loop(first, 10 - first, lambda r: conv_in(wo_in[layer], ohid, r))
        rows = []
        for r in range(first + 1, 9 - first):
            y = conv_out(wo_out[layer], ohid, r)
            row = ((st[r, 0:40] + y[0:40]) * st[r, 40:41]).astype(BF16)
            if layer == 0:
                row = row.astype(F32) * jnp.where(valid(r), 1.0, 0.0)
                st[r, 0:40] = row
                put_taps(r, jnp.concatenate([row, flux_row(r)], axis=0))
            else:
                orows.append(row[:, 0:384])
                rows.append(row[0:16, 0:384].astype(F32)[0:1])
        temp = rows

    warm = [
        jnp.broadcast_to(temp[b // 3][:, (b % 3) * 128 : (b % 3 + 1) * 128], (16, 128))
        for b in range(6)
    ]
    b_start, b_wait, b_done = swap(bs, br, b_s, b_r)
    for p in range(nt):
        target = tq[p].astype(F32)
        back = jnp.zeros((16, 128), F32)
        for b in range(6):
            back = jnp.where(target == b, warm[b], back)
        bs[p] = back.astype(BF16)
    b_start()
    onext_ref[...] = jnp.stack([v.astype(F32) for v in orows], axis=1).astype(BF16)
    halos[0][2]()
    halos[1][2]()
    tq_done()
    c_done()
    f_done()
    heat = [jnp.zeros((8, 128), F32) for b in range(6)]
    for p in [t] + peers:
        if p is not t:
            b_wait(p)
        got = br[p].astype(F32)
        for s in range(2):
            piece = lax.dot_general(
                got[8 * s : 8 * s + 8].astype(BF16),
                blk_v[wgt_ref[s, p]],
                (((1,), (1,)), ((), ())),
                preferred_element_type=F32,
            )
            source = jnp.full((8, 128), src_ref[s, p], jnp.int32)
            for b in range(6):
                heat[b] = heat[b] + jnp.where(source == b, piece, 0.0)
    for b in range(6):
        temp_ref[b // 3 : b // 3 + 1, (b % 3) * 128 : (b % 3 + 1) * 128] = heat[b][0:1]

    b_done()


def hand_out_kernel(*refs):
    sems = refs[6]
    copies = [
        pltpu.make_async_copy(source, target, sems.at[i])
        for i, (source, target) in enumerate(zip(refs[:3], refs[3:6]))
    ]
    for copy in copies:
        copy.start()
    for copy in copies:
        copy.wait()


def hand_out(*arrays):
    vmem = pl.BlockSpec(memory_space=pltpu.VMEM)
    return pl.pallas_call(
        hand_out_kernel,
        out_shape=tuple(jax.ShapeDtypeStruct(v.shape, v.dtype) for v in arrays),
        in_specs=[vmem] * 3,
        out_specs=(pl.BlockSpec(memory_space=pltpu.HBM),) * 3,
        scratch_shapes=[pltpu.SemaphoreType.DMA((3,))],
    )(*[pltpu.with_memory_space_constraint(v, pltpu.VMEM) for v in arrays])


def per_device(
    dims,
    atmos_state,
    ocean_state,
    ocean_mask,
    atmos_in_w,
    atmos_out_w,
    ocean_in_w,
    ocean_out_w,
    flux_proj,
    regrid_blocks,
    regrid_source_block,
    regrid_target_block,
    regrid_weight_block,
):
    nt, nc, nl = dims
    sides = 1 if nl == 2 else 2
    in_taps = [w.transpose(0, 1, 3, 2) for w in (atmos_in_w, ocean_in_w)]
    links = [
        v.reshape(nt, 2).T
        for v in (regrid_source_block, regrid_target_block, regrid_weight_block)
    ]
    vmem = pl.BlockSpec(memory_space=pltpu.VMEM)
    hbm = pl.BlockSpec(memory_space=pltpu.HBM)
    dma = pltpu.SemaphoreType.DMA
    anext, onext, temp = pl.pallas_call(
        functools.partial(kernel, dims),
        out_shape=(
            pltpu.VMEM((48, 2, 384), BF16),
            pltpu.VMEM((40, 2, 384), BF16),
            pltpu.VMEM((2, 384), F32),
        ),
        in_specs=[hbm] * 12,
        out_specs=(vmem, vmem, vmem),
        scratch_shapes=[
            pltpu.SMEM((2, nt), jnp.int32),
            pltpu.SMEM((2, nt), jnp.int32),
            pltpu.SMEM((2, nt), jnp.int32),
            pltpu.VMEM(atmos_state.shape, BF16),
            pltpu.VMEM(ocean_state.shape, BF16),
            pltpu.VMEM(ocean_mask.shape, jnp.int32),
            pltpu.VMEM(flux_proj.shape, BF16),
            pltpu.VMEM(in_taps[0].shape, BF16),
            pltpu.VMEM(atmos_out_w.shape, BF16),
            pltpu.VMEM(in_taps[1].shape, BF16),
            pltpu.VMEM(ocean_out_w.shape, BF16),
            pltpu.VMEM(regrid_blocks.shape, BF16),
            pltpu.VMEM((2, 256, 432), BF16),
            pltpu.VMEM((2, 144, 768), BF16),
            pltpu.VMEM((2, 128, 432), BF16),
            pltpu.VMEM((2, 144, 384), BF16),
            pltpu.VMEM((2, 5, 2, 48, 384), BF16),
            pltpu.VMEM((2, 16, 128), BF16),
            pltpu.VMEM((2, sides, 5, 16, 128), BF16),
            pltpu.VMEM((10, 144, WIDE), BF16),
            pltpu.VMEM((10, 32, WIDE), BF16),
            pltpu.VMEM((8, 128, WIDE), F32),
            pltpu.VMEM((128, 96), BF16),
            pltpu.VMEM((8, 256, WIDE), BF16),
            pltpu.VMEM((8, 128, WIDE), BF16),
            pltpu.VMEM((10, 48, WIDE), F32),
            pltpu.VMEM((5, 16, 384), BF16),
            pltpu.VMEM((16, 128), BF16),
            pltpu.VMEM((sides, 5, 16, 128), BF16),
            pltpu.VMEM((nt, 16, 128), BF16),
            pltpu.VMEM((nt, 16, 128), BF16),
            pltpu.VMEM((nt, 16, 128), BF16),
            pltpu.VMEM((nt, 16, 128), BF16),
            pltpu.VMEM((nt, 16, 128), BF16),
            pltpu.VMEM((nt, 16, 128), BF16),
            dma((5,)),
            dma((7,)),
            dma((2, 5)),
            dma((2, 5)),
            dma((2, sides, 5)),
            dma((2, sides, 5)),
            dma((5,)),
            dma((5,)),
            dma((sides, 5)),
            dma((sides, 5)),
            dma((nt,)),
            dma((nt,)),
            dma((nt,)),
            dma((nt,)),
            dma((nt,)),
            dma((nt,)),
        ],
        compiler_params=pltpu.CompilerParams(
            collective_id=0, has_side_effects=True, vmem_limit_bytes=60 * 1024 * 1024
        ),
    )(
        *links,
        atmos_state,
        ocean_state,
        ocean_mask,
        flux_proj,
        in_taps[0],
        atmos_out_w,
        in_taps[1],
        ocean_out_w,
        regrid_blocks,
    )
    return hand_out(anext, onext, temp)


def solution(mesh):
    dims = (mesh.shape["lat"] * mesh.shape["comp"], mesh.shape["comp"], mesh.shape["lon"])
    field = P(None, ("grp", "lat", "comp"), "lon")
    plane = P(("grp", "lat", "comp"), "lon")
    links = P(("grp", "lat", "comp"), "lon", None, None)
    in_specs = (field, field, plane) + (P(),) * 6 + (links,) * 3
    return jax.shard_map(
        functools.partial(per_device, dims),
        mesh=mesh,
        in_specs=in_specs,
        out_specs=(field, field, plane),
        check_vma=False,
    )
```

```python
import functools

import jax
import jax.numpy as jnp
from jax import lax
from jax.experimental import pallas as pl
from jax.experimental.pallas import tpu as pltpu
from jax.sharding import PartitionSpec as P

MESH = pl.DeviceIdType.MESH
F32 = jnp.float32
BF16 = jnp.bfloat16
WIDE = 512
NEAR = (0, 1, -1)
FAR = (2, -2)


def gelu(v, keep):
    v = v.astype(BF16)
    half = (0.5 * keep).astype(BF16) * v
    slope = jnp.asarray(0.7978845608 * 0.044715, BF16) * (v * v)
    return half + half * jnp.tanh(v * (jnp.asarray(0.7978845608, BF16) + slope))


def kernel(
    dims,
    src_hbm,
    tgt_hbm,
    wgt_hbm,
    atmos_hbm,
    ocean_hbm,
    mask_hbm,
    proj_hbm,
    ain_hbm,
    aout_hbm,
    oin_hbm,
    oout_hbm,
    blk_hbm,
    anext_ref,
    onext_ref,
    temp_ref,
    src_ref,
    tgt_ref,
    wgt_ref,
    atmos_ref,
    ocean_ref,
    mask_ref,
    proj_ref,
    ain_v,
    aout_v,
    oin_v,
    oout_v,
    blk_v,
    wa_in,
    wa_out,
    wo_in,
    wo_out,
    main,
    rim,
    edge,
    xp,
    xf,
    pre,
    wo_flux,
    hid,
    ohid,
    st,
    fmain,
    fedge_src,
    fedge,
    tq_src,
    tq,
    cs,
    cr,
    bs,
    br,
    w_sem,
    i_sem,
    ms,
    mr,
    es,
    er,
    fms,
    fmr,
    fes,
    fer,
    tqs,
    tqr,
    c_s,
    c_r,
    b_s,
    b_r,
):
    nt, nc, nl = dims
    comp = lax.axis_index("comp")
    lat = lax.axis_index("lat")
    lon = lax.axis_index("lon")
    t = lat * nc + comp
    sides = (1,) if nl == 2 else (1, nl - 1)

    def dev(tt, ll):
        return {"lat": lax.div(tt, nc), "comp": lax.rem(tt, nc), "lon": ll}

    upper = lax.div(t, nt // 2)

    def near_first(i):
        return i + upper * (nt - 1 - 2 * i)

    def inside(d):
        return (t + d >= 0) & (t + d < nt)

    barrier = pltpu.get_barrier_semaphore()
    for k in range(1, nt):
        pl.semaphore_signal(
            barrier, inc=1, device_id=dev(lax.rem(t + k, nt), lon), device_id_type=MESH
        )
    for e in range(-2, 3):

        @pl.when(inside(e))
        def _():
            for s in sides:
                pl.semaphore_signal(
                    barrier,
                    inc=1,
                    device_id=dev(t + e, lax.rem(lon + s, nl)),
                    device_id_type=MESH,
                )

    input_copies = [
        pltpu.make_async_copy(src, dst, i_sem.at[i])
        for i, (src, dst) in enumerate(
            (
                (atmos_hbm, atmos_ref),
                (tgt_hbm, tgt_ref),
                (ocean_hbm, ocean_ref),
                (mask_hbm, mask_ref),
                (src_hbm, src_ref),
                (wgt_hbm, wgt_ref),
                (proj_hbm, proj_ref),
            )
        )
    ]
    for copy in input_copies:
        copy.start()
    weight_copies = [
        pltpu.make_async_copy(src, dst, w_sem.at[i])
        for i, (src, dst) in enumerate(
            (
                (ain_hbm, ain_v),
                (aout_hbm, aout_v),
                (blk_hbm, blk_v),
                (oin_hbm, oin_v),
                (oout_hbm, oout_v),
            )
        )
    ]
    for copy in weight_copies:
        copy.start()
    lane = lax.broadcasted_iota(jnp.int32, (16, 128), 1)

    def own_rows(m, rows):
        for i in range(2):
            main[m, 2, i] = rows[i].astype(BF16)

    def own_rim(m, rows):
        packed = jnp.zeros((16, 128), F32)
        for i in range(2):
            for g in range(3):
                q = i * 3 + g
                part = rows[i][16 * g : 16 * g + 16]
                ends = jnp.where(lane < 64, part[:, 0:128], part[:, 256:384])
                moved = pltpu.roll(ends, 16 * q + 8, 1)
                packed = jnp.where((lane >= 16 * q) & (lane < 16 * q + 16), moved, packed)
        rim[m] = packed.astype(BF16)

    def exchange(main_src, main_dst, edge_src, edge_dst, msend, mrecv, esend, erecv):
        def main_copy(e, out):
            j = 2 - e if out else e + 2
            return pltpu.make_async_remote_copy(
                src_ref=main_src,
                dst_ref=main_dst.at[j],
                send_sem=msend.at[e + 2],
                recv_sem=mrecv.at[j],
                device_id=dev(t + e, lon),
                device_id_type=MESH,
            )

        def edge_copy(e, n, s, out):
            j = 2 - e if out else e + 2
            return pltpu.make_async_remote_copy(
                src_ref=edge_src,
                dst_ref=edge_dst.at[n, j],
                send_sem=esend.at[n, e + 2],
                recv_sem=erecv.at[n, j],
                device_id=dev(t + e, lax.rem(lon + s, nl)),
                device_id_type=MESH,
            )

        def start():
            for places in ((-1, 1, 0), (-2, 2)):
                for e in places:

                    @pl.when(inside(e))
                    def _():
                        for n, s in enumerate(sides):
                            edge_copy(e, n, s, True).start()

                for e in places:
                    if e != 0:

                        @pl.when(inside(e))
                        def _():
                            main_copy(e, True).start()

        def wait_recv(places):
            for d in places:

                @pl.when(inside(d))
                def _():
                    for n, s in enumerate(sides):
                        edge_copy(d, n, s, False).wait_recv()
                    if d != 0:
                        main_copy(d, False).wait_recv()

                if d != 0:

                    @pl.when(jnp.logical_not(inside(d)))
                    def _():
                        main_dst[d + 2] = jnp.zeros(main_dst.shape[1:], main_dst.dtype)
                        for n in range(len(sides)):
                            edge_dst[n, d + 2] = jnp.zeros(edge_dst.shape[2:], edge_dst.dtype)

        def wait_send():
            for e in (-2, 2, -1, 1, 0):

                @pl.when(inside(e))
                def _():
                    if e != 0:
                        main_copy(e, True).wait_send()
                    for n, s in enumerate(sides):
                        edge_copy(e, n, s, True).wait_send()

        return start, wait_recv, wait_send

    def swap(src, dst, ssem, rsem):
        def copy(p, out):
            return pltpu.make_async_remote_copy(
                src_ref=src.at[p],
                dst_ref=dst.at[t if out else p],
                send_sem=ssem.at[p],
                recv_sem=rsem.at[t if out else p],
                device_id=dev(jnp.int32(p), lon),
                device_id_type=MESH,
            )

        def start(p):
            @pl.when(t != p)
            def _():
                copy(p, True).start()

            @pl.when(t == p)
            def _():
                dst[p] = src[p]

        def wait_recv(p):
            @pl.when(t != p)
            def _():
                copy(p, False).wait_recv()

        def wait_send():
            for p in range(nt):

                @pl.when(t != p)
                def _():
                    copy(p, True).wait_send()

        return start, wait_recv, wait_send

    halos = [
        exchange(
            main.at[m, 2],
            main.at[m],
            rim.at[m],
            edge.at[m],
            ms.at[m],
            mr.at[m],
            es.at[m],
            er.at[m],
        )
        for m in range(2)
    ]
    input_copies[0].wait()
    atmos_rows = [atmos_ref[:, i, :].astype(F32) for i in range(2)]
    own_rows(0, atmos_rows)
    own_rim(0, atmos_rows)
    low = jnp.minimum(t, 2)
    high = jnp.minimum(nt - 1 - t, 2)
    pl.semaphore_wait(barrier, nt - 1 + len(sides) * (low + high + 1))
    halos[0][0]()
    input_copies[1].wait()
    for p in range(nt):
        tq_src[p] = jnp.concatenate(
            [jnp.full((8, 128), tgt_ref[s, p], jnp.int32) for s in range(2)], axis=0
        ).astype(F32).astype(BF16)
    for copy in input_copies[2:]:
        copy.wait()
    wet = mask_ref[...].astype(F32)
    ocean_rows = [
        jnp.concatenate(
            [
                ocean_ref[:, i, :].astype(F32) * wet[i : i + 1],
                jnp.broadcast_to(wet[i : i + 1], (8, 384)),
            ],
            axis=0,
        )
        for i in range(2)
    ]
    own_rows(1, ocean_rows)
    own_rim(1, ocean_rows)
    tq_start, tq_wait, tq_done = swap(tq_src, tq, tqs, tqr)

    def stack_in(src, dst):
        for k in range(2):
            dst[k] = src[k].reshape(432, src.shape[3]).T

    def stack_out(src, dst, c, h):
        for k in range(2):
            for a in range(3):
                for b in range(3):
                    dst[k, b * 48 : b * 48 + c, a * h : (a + 1) * h] = src[k, 3 * a + b]

    weight_copies[0].wait()
    stack_in(ain_v, wa_in)
    weight_copies[1].wait()
    stack_out(aout_v, wa_out, 48, 256)

    def valid(r):
        row = 2 * t + r - 4
        return (row >= 0) & (row < 2 * nt)

    def wide_row(m, r):
        j, i = r // 2, r % 2
        pieces = []
        for g in range(3):
            shift = (120 - (i * 3 + g) * 16) % 128
            got = [pltpu.roll(edge[m, n, j].astype(F32), shift, 1) for n in range(len(sides))]
            pieces.append(got[0] if len(got) == 1 else jnp.where(lane < 64, got[1], got[0]))
        return jnp.concatenate(
            [main[m, j, i].astype(F32), jnp.concatenate(pieces, axis=0)], axis=1
        )

    def put_taps(r, row):
        row = row.astype(BF16)
        xp[r, 0:48] = pltpu.roll(row, 1, 1)
        xp[r, 48:96] = row
        xp[r, 96:144] = pltpu.roll(row, WIDE - 1, 1)

    def conv_in(w, buf, r):
        patch = xp[pl.ds(r - 1, 3)].reshape(432, WIDE)
        v = jnp.dot(w, patch, preferred_element_type=F32)
        buf[r - 1] = gelu(v, jnp.where(valid(r), 1.0, 0.0)).astype(BF16)

    def conv_out(w, buf, r):
        h = buf.shape[1]
        y = jnp.dot(w, buf[pl.ds(r - 2, 3)].reshape(3 * h, WIDE), preferred_element_type=F32)
        before, after = y[0:48].astype(BF16), y[96:144].astype(BF16)
        beside = pltpu.roll(before, 1, 1).astype(F32) + pltpu.roll(after, WIDE - 1, 1).astype(F32)
        return y[48:96] + beside

    def loop(lo, hi, fn):
        for r in range(lo, hi):
            fn(r)

    def load_rows(rows):
        for r in rows:
            row = wide_row(0, r)
            put_taps(r, row)
            if 2 <= r < 8:
                st[r] = row

    halos[0][1](NEAR)
    load_rows(range(2, 8))
    loop(3, 7, lambda r: conv_in(wa_in[0], hid, r))
    halos[1][0]()
    halos[0][1](FAR)
    for i in range(nt):
        tq_start(near_first(i))
    load_rows((0, 1, 8, 9))

    arows, orows = [], []
    for layer in range(2):
        first = 1 + 2 * layer

        for r in (1, 2, 7, 8) if layer == 0 else range(3, 7):
            conv_in(wa_in[layer], hid, r)
        for r in range(first + 1, 9 - first):
            row = (st[r] + conv_out(wa_out[layer], hid, r)).astype(BF16)
            if layer == 0:
                row = row.astype(F32) * jnp.where(valid(r), 1.0, 0.0)
                st[r] = row
                put_taps(r, row)
            else:
                arows.append(row[:, 0:384])

    flux = [
        jnp.dot(proj_ref[...], arows[i], preferred_element_type=F32).astype(BF16).astype(F32)
        for i in range(2)
    ]
    sub = [flux[b // 3][:, (b % 3) * 128 : (b % 3 + 1) * 128] for b in range(6)]
    weight_copies[2].wait()
    c_start, c_wait, c_done = swap(cs, cr, c_s, c_r)
    for i in range(nt):
        p = near_first(nt - 1 - i)
        out = []
        for s in range(2):
            source = jnp.full((8, 128), src_ref[s, p], jnp.int32)
            chosen = jnp.zeros((8, 128), F32)
            for b in range(6):
                chosen = jnp.where(source == b, sub[b], chosen)
            out.append(
                jnp.dot(
                    chosen.astype(BF16),
                    blk_v[wgt_ref[s, p]],
                    preferred_element_type=F32,
                )
            )
        cs[p] = jnp.concatenate(out, axis=0).astype(BF16)
        c_start(p)

    anext_ref[...] = jnp.stack([v.astype(F32) for v in arows], axis=1).astype(BF16)
    weight_copies[3].wait()
    stack_in(oin_v, wo_in)
    weight_copies[4].wait()
    wo_out[...] = jnp.zeros(wo_out.shape, BF16)
    stack_out(oout_v, wo_out, 40, 128)
    halos[1][1](NEAR + FAR)
    taps = [oin_v[0, tap].astype(F32)[40:48] for tap in range(9)]
    gap = [jnp.zeros((8, 128), F32)]
    wo_flux[...] = (
        jnp.concatenate(taps[0:3] + gap + taps[3:6] + gap + taps[6:9] + gap, axis=0).astype(BF16).T
    )
    for r in range(10):
        row = wide_row(1, r)
        st[r] = row
        put_taps(r, jnp.concatenate([row[0:40], jnp.zeros((8, WIDE), F32)], axis=0))

    def pre_in(r):
        patch = xp[r - 1 : r + 2].reshape(432, WIDE)
        pre[r - 1] = jnp.dot(wo_in[0], patch, preferred_element_type=F32)

    for r in range(1, 5):
        pre_in(r)
    for p in range(nt):
        tq_wait(p)

    total = [jnp.zeros((8, 128), F32) for b in range(6)]
    for i in range(nt):
        p = near_first(i)
        c_wait(p)
        arrived = cr[p].astype(F32)
        target = tq[p].astype(F32)
        for s in range(2):
            value, where_to = arrived[8 * s : 8 * s + 8], target[8 * s : 8 * s + 8]
            for b in range(6):
                total[b] = total[b] + jnp.where(where_to == b, value, 0.0)
    own = jnp.concatenate(
        [jnp.concatenate(total[0:3], axis=1), jnp.concatenate(total[3:6], axis=1)], axis=0
    )
    fmain[2] = own.astype(BF16)
    fedge_src[...] = jnp.where(lane < 64, own[:, 0:128], own[:, 256:384]).astype(BF16)
    f_start, f_wait, f_done = exchange(
        fmain.at[2], fmain, fedge_src, fedge, fms, fmr, fes, fer
    )
    f_start()
    for r in range(5, 9):
        pre_in(r)
    def flux_row(r):
        j, i = r // 2, r % 2
        got = [fedge[n, j].astype(F32) for n in range(len(sides))]
        side = got[0] if len(got) == 1 else jnp.where(lane < 64, got[1], got[0])
        both = jnp.concatenate([fmain[j].astype(F32), side], axis=1)
        return both[8 * i : 8 * i + 8]

    def flux_taps(rows):
        for r in rows:
            row = flux_row(r)
            xf[r] = jnp.concatenate(
                [
                    pltpu.roll(row, 1, 1),
                    row,
                    pltpu.roll(row, WIDE - 1, 1),
                    jnp.zeros((8, WIDE), F32),
                ],
                axis=0,
            ).astype(BF16)

    temp = None

    def flux_in(r):
        v = pre[r - 1] + jnp.dot(
            wo_flux[...], xf[r - 1 : r + 2].reshape(96, WIDE), preferred_element_type=F32
        )
        ohid[r - 1] = gelu(v, jnp.where(valid(r), 1.0, 0.0)).astype(BF16)
    for layer in range(2):
        first = 1 + 2 * layer

        if layer == 0:
            f_wait(NEAR)
            flux_taps(range(2, 8))
            loop(3, 7, flux_in)
            f_wait(FAR)
            flux_taps((0, 1, 8, 9))
            for r in (1, 2, 7, 8):
                flux_in(r)
        else:
            loop(first, 10 - first, lambda r: conv_in(wo_in[layer], ohid, r))
        rows = []
        for r in range(first + 1, 9 - first):
            y = conv_out(wo_out[layer], ohid, r)
            row = ((st[r, 0:40] + y[0:40]) * st[r, 40:41]).astype(BF16)
            if layer == 0:
                row = row.astype(F32) * jnp.where(valid(r), 1.0, 0.0)
                st[r, 0:40] = row
                put_taps(r, jnp.concatenate([row, flux_row(r)], axis=0))
            else:
                orows.append(row[:, 0:384])
                rows.append(row[0:16, 0:384].astype(F32)[0:1])
        temp = rows

    warm = [
        jnp.broadcast_to(temp[b // 3][:, (b % 3) * 128 : (b % 3 + 1) * 128], (16, 128))
        for b in range(6)
    ]
    b_start, b_wait, b_done = swap(bs, br, b_s, b_r)
    for i in range(nt):
        p = near_first(nt - 1 - i)
        target = tq[p].astype(F32)
        back = jnp.zeros((16, 128), F32)
        for b in range(6):
            back = jnp.where(target == b, warm[b], back)
        bs[p] = back.astype(BF16)
        b_start(p)
    onext_ref[...] = jnp.stack([v.astype(F32) for v in orows], axis=1).astype(BF16)
    halos[0][2]()
    halos[1][2]()
    tq_done()
    c_done()
    f_done()
    heat = [jnp.zeros((8, 128), F32) for b in range(6)]
    for i in range(nt):
        p = near_first(i)
        b_wait(p)
        got = br[p].astype(F32)
        for s in range(2):
            piece = lax.dot_general(
                got[8 * s : 8 * s + 8].astype(BF16),
                blk_v[wgt_ref[s, p]],
                (((1,), (1,)), ((), ())),
                preferred_element_type=F32,
            )
            source = jnp.full((8, 128), src_ref[s, p], jnp.int32)
            for b in range(6):
                heat[b] = heat[b] + jnp.where(source == b, piece, 0.0)
    for b in range(6):
        temp_ref[b // 3 : b // 3 + 1, (b % 3) * 128 : (b % 3 + 1) * 128] = heat[b][0:1]

    b_done()


def hand_out_kernel(*refs):
    sems = refs[6]
    copies = [
        pltpu.make_async_copy(source, target, sems.at[i])
        for i, (source, target) in enumerate(zip(refs[:3], refs[3:6]))
    ]
    for copy in copies:
        copy.start()
    for copy in copies:
        copy.wait()


def hand_out(*arrays):
    vmem = pl.BlockSpec(memory_space=pltpu.VMEM)
    return pl.pallas_call(
        hand_out_kernel,
        out_shape=tuple(jax.ShapeDtypeStruct(v.shape, v.dtype) for v in arrays),
        in_specs=[vmem] * 3,
        out_specs=(pl.BlockSpec(memory_space=pltpu.HBM),) * 3,
        scratch_shapes=[pltpu.SemaphoreType.DMA((3,))],
    )(*[pltpu.with_memory_space_constraint(v, pltpu.VMEM) for v in arrays])


def per_device(
    dims,
    atmos_state,
    ocean_state,
    ocean_mask,
    atmos_in_w,
    atmos_out_w,
    ocean_in_w,
    ocean_out_w,
    flux_proj,
    regrid_blocks,
    regrid_source_block,
    regrid_target_block,
    regrid_weight_block,
):
    nt, nc, nl = dims
    sides = 1 if nl == 2 else 2
    in_taps = [w.transpose(0, 1, 3, 2) for w in (atmos_in_w, ocean_in_w)]
    links = [
        v.reshape(nt, 2).T
        for v in (regrid_source_block, regrid_target_block, regrid_weight_block)
    ]
    vmem = pl.BlockSpec(memory_space=pltpu.VMEM)
    hbm = pl.BlockSpec(memory_space=pltpu.HBM)
    dma = pltpu.SemaphoreType.DMA
    anext, onext, temp = pl.pallas_call(
        functools.partial(kernel, dims),
        out_shape=(
            pltpu.VMEM((48, 2, 384), BF16),
            pltpu.VMEM((40, 2, 384), BF16),
            pltpu.VMEM((2, 384), F32),
        ),
        in_specs=[hbm] * 12,
        out_specs=(vmem, vmem, vmem),
        scratch_shapes=[
            pltpu.SMEM((2, nt), jnp.int32),
            pltpu.SMEM((2, nt), jnp.int32),
            pltpu.SMEM((2, nt), jnp.int32),
            pltpu.VMEM(atmos_state.shape, BF16),
            pltpu.VMEM(ocean_state.shape, BF16),
            pltpu.VMEM(ocean_mask.shape, jnp.int32),
            pltpu.VMEM(flux_proj.shape, BF16),
            pltpu.VMEM(in_taps[0].shape, BF16),
            pltpu.VMEM(atmos_out_w.shape, BF16),
            pltpu.VMEM(in_taps[1].shape, BF16),
            pltpu.VMEM(ocean_out_w.shape, BF16),
            pltpu.VMEM(regrid_blocks.shape, BF16),
            pltpu.VMEM((2, 256, 432), BF16),
            pltpu.VMEM((2, 144, 768), BF16),
            pltpu.VMEM((2, 128, 432), BF16),
            pltpu.VMEM((2, 144, 384), BF16),
            pltpu.VMEM((2, 5, 2, 48, 384), BF16),
            pltpu.VMEM((2, 16, 128), BF16),
            pltpu.VMEM((2, sides, 5, 16, 128), BF16),
            pltpu.VMEM((10, 144, WIDE), BF16),
            pltpu.VMEM((10, 32, WIDE), BF16),
            pltpu.VMEM((8, 128, WIDE), F32),
            pltpu.VMEM((128, 96), BF16),
            pltpu.VMEM((8, 256, WIDE), BF16),
            pltpu.VMEM((8, 128, WIDE), BF16),
            pltpu.VMEM((10, 48, WIDE), F32),
            pltpu.VMEM((5, 16, 384), BF16),
            pltpu.VMEM((16, 128), BF16),
            pltpu.VMEM((sides, 5, 16, 128), BF16),
            pltpu.VMEM((nt, 16, 128), BF16),
            pltpu.VMEM((nt, 16, 128), BF16),
            pltpu.VMEM((nt, 16, 128), BF16),
            pltpu.VMEM((nt, 16, 128), BF16),
            pltpu.VMEM((nt, 16, 128), BF16),
            pltpu.VMEM((nt, 16, 128), BF16),
            dma((5,)),
            dma((7,)),
            dma((2, 5)),
            dma((2, 5)),
            dma((2, sides, 5)),
            dma((2, sides, 5)),
            dma((5,)),
            dma((5,)),
            dma((sides, 5)),
            dma((sides, 5)),
            dma((nt,)),
            dma((nt,)),
            dma((nt,)),
            dma((nt,)),
            dma((nt,)),
            dma((nt,)),
        ],
        compiler_params=pltpu.CompilerParams(
            collective_id=0, has_side_effects=True, vmem_limit_bytes=60 * 1024 * 1024
        ),
    )(
        *links,
        atmos_state,
        ocean_state,
        ocean_mask,
        flux_proj,
        in_taps[0],
        atmos_out_w,
        in_taps[1],
        ocean_out_w,
        regrid_blocks,
    )
    return hand_out(anext, onext, temp)


def solution(mesh):
    dims = (mesh.shape["lat"] * mesh.shape["comp"], mesh.shape["comp"], mesh.shape["lon"])
    field = P(None, ("grp", "lat", "comp"), "lon")
    plane = P(("grp", "lat", "comp"), "lon")
    links = P(("grp", "lat", "comp"), "lon", None, None)
    in_specs = (field, field, plane) + (P(),) * 6 + (links,) * 3
    return jax.shard_map(
        functools.partial(per_device, dims),
        mesh=mesh,
        in_specs=in_specs,
        out_specs=(field, field, plane),
        check_vma=False,
    )
```
